32 devices in a mesh: dp: 2 (over core), expert: 4 (over y, x), mp: 4 (over z).
Axes of the slice: x: 2, y: 2, z: 4, core: 2. Of those that a mesh axis runs over, the one named last changes fastest.
Arguments:
- tokens: bfloat16 [512, 3072], P(('dp', 'expert')), may hold values from -6 to 6
- w_router: float32 [3072, 4], replicated, may hold values from -0.109375 to 0.109375
- expert_ids: int32 [512, 2], P(('dp', 'expert')), may hold values from 0 to 3, all different within a row; in each aligned block of 64 rows (0 to 63, 64 to 127, ...) at most 64 rows name the same one
- partner: int32 [4], replicated, may hold values from 0 to 3, as said below
- gate_weight: bfloat16 [4, 3072, 8192], P('expert', None, ('dp', 'mp')), may hold values from -0.109375 to 0.109375
- up_weight: bfloat16 [4, 3072, 8192], P('expert', None, ('dp', 'mp')), may hold values from -0.109375 to 0.109375
- down_weight: bfloat16 [4, 8192, 3072], P('expert', ('dp', 'mp')), may hold values from -0.0625 to 0.0625
- grad_out: bfloat16 [512, 3072], P(('dp', 'expert')), may hold values from -1.5 to 1.5
Outputs:
- mixed: bfloat16 [512, 3072], P(('dp', 'expert'))
- grad_tokens: bfloat16 [512, 3072], P(('dp', 'expert'))
- grad_router: float32 [3072, 4], replicated
- grad_gate: bfloat16 [4, 3072, 8192], P('expert', None, ('dp', 'mp'))
- grad_up: bfloat16 [4, 3072, 8192], P('expert', None, ('dp', 'mp'))
- grad_down: bfloat16 [4, 8192, 3072], P('expert', ('dp', 'mp'))
The draws below stay inside these ranges and needn't reach their ends.
Inputs may be any that keep to these rules, and one draw needn't show every extreme that they name: `expert_ids`: each token names two different experts. Within each aligned block of 64 tokens no expert is named by more than 64 tokens, and in every draw some block names some expert exactly 64 times. A matching of the experts: partner[partner[e]] = e and partner[e] != e for every expert e.
All inputs are finite; a program needn't handle non-finite values.
Results may differ from the reference program's by a relative error of at most 0.019.
Values may be sent and summed in bfloat16 or wider, within the bound.
No kernel may reach another device: no remote copies, remote signals or barrier semaphores. Data moves between devices by JAX's collectives and lax.ppermute only.
A program may use at most 128 MiB of HBM per device.

```python
import math
import jax
import jax.numpy as jnp
import numpy as np
from jax import lax

D = 3072
FF = 8192
TOK_DEV = 64
EXPERTS = 4
TOKENS = 512
MOST = 64
CAP = 48
N_DP = 2
N_MP = 4


def draw_partner(key, part):
    shuffled = jax.random.permutation(key, EXPERTS).astype(jnp.int32)
    where_at = jnp.argsort(shuffled).astype(jnp.int32)
    mate_pos = jnp.bitwise_xor(where_at, 1)
    return shuffled[mate_pos].astype(jnp.int32)


def levels(key, extent, split, smallest, largest):
    loudness, own = 1.0, jax.random.fold_in(key, 6)
    for dim, parts in split:
        heights = jnp.exp(jax.random.uniform(jax.random.fold_in(own, dim), (parts,), jnp.float32, smallest / len(split), largest / len(split)))
        loudness = loudness * jnp.repeat(heights, extent[dim] // parts).reshape([-1 if axis == dim else 1 for axis in range(len(extent))])
    return loudness


def shared_out(key, own, number, rows, amount, top, most, skew):
    ranking = jax.random.permutation(key, amount)
    heavy_load, common = load_shares(amount, rows * top, most, skew, True), load_shares(amount, rows * top, most, skew, False)
    places = jnp.arange(amount)

    def named(lengths, turn):
        used = int((lengths > 0).sum())
        fixed = max(1, used // 4)
        moved = fixed + (places - fixed + turn * (used - fixed)) % max(1, amount - fixed)
        return jnp.zeros((amount,), jnp.int32).at[ranking[jnp.where(places < fixed, places, moved)]].set(jnp.asarray(lengths, jnp.int32))

    lengths = jnp.where(number % 4 == 0, named(heavy_load, number // 4), named(common, number - number // 4 - 1))
    mixed = jax.random.permutation(jax.random.fold_in(own, 3), amount)
    giver, sink = mixed[0:amount // 2 * 2:2], mixed[1:amount // 2 * 2:2]
    room = jnp.minimum(lengths[giver] - 1, most - lengths[sink]) // 2
    room = jnp.where((giver == ranking[0]) | (sink == ranking[0]) | (lengths[sink] == 0), 0, jnp.maximum(room, 0))
    moved = jax.random.randint(jax.random.fold_in(own, 4), (amount // 2,), 0, 1 << 20) % (room + 1)
    lengths = lengths.at[giver].add(-moved).at[sink].add(moved)
    members = jnp.searchsorted(jnp.cumsum(lengths), jnp.arange(rows * top), side="right").astype(jnp.int32)
    listing = members.reshape(top, rows).T
    listing = listing[jax.random.permutation(jax.random.fold_in(own, 1), rows)]
    turn = jax.random.randint(jax.random.fold_in(own, 2), (rows, 1), 0, top)
    return jnp.take_along_axis(listing, (jnp.arange(top)[None, :] + turn) % top, axis=1)


def load_shares(amount, total, reach, slope, full):
    portions = [(1 << 20) // math.isqrt(rank ** slope) + 1 for rank in range(1, amount + 1)]
    largest = reach if full else min(reach, max(-(-total // amount), total * portions[0] // sum(portions)))
    least = 1 if total - largest >= amount - 1 else 0
    given, rest = [largest] + [least] * (amount - 1), total - largest - least * (amount - 1)
    while rest > 0:
        free = [i for i in range(1, amount) if given[i] < largest] or [i for i in range(1, amount) if given[i] < reach]
        whole, budget = sum([portions[i] for i in free]), rest
        for i in free:
            addition = min(reach - given[i], max(1, budget * portions[i] // whole), rest)
            given[i] = given[i] + addition
            rest = rest - addition
    return np.array(given)


def gaussian(key, dims, deviation, reach, shards=(), held_as=jnp.bfloat16):
    values = deviation * jax.random.normal(key, dims, jnp.float32)
    if shards:
        values = values * levels(key, dims, shards, -0.22, 0.18)
    return jnp.clip(values, -reach, reach).astype(held_as)


def setup_inputs(seed: int = 0) -> dict:
    seeds = jax.random.split(jax.random.key(seed), 9)
    tokens = gaussian(seeds[0], (TOKENS, D), 1.0, 6.0, ((0, 8),))
    w_router = gaussian(seeds[1], (D, EXPERTS), D ** -0.5, 0.109375, (), jnp.float32)
    expert_ids_keys = jax.random.split(jax.random.fold_in(seeds[2], 1), TOKENS // TOK_DEV)
    expert_ids_turns = jax.random.permutation(jax.random.fold_in(seeds[2], 3), TOKENS // TOK_DEV)
    expert_ids = jax.vmap(lambda own, number: shared_out(jax.random.fold_in(seeds[2], 2), own, number, TOK_DEV, EXPERTS, 2, MOST, 2))(expert_ids_keys, expert_ids_turns).reshape((TOKENS, 2))
    partner = draw_partner(jax.random.fold_in(seeds[8], 71), 0)
    gate_weight = gaussian(seeds[4], (EXPERTS, D, FF), D ** -0.5, 0.109375, ((0, 4), (2, 8)))
    up_weight = gaussian(seeds[5], (EXPERTS, D, FF), D ** -0.5, 0.109375, ((0, 4), (2, 8)))
    down_weight = gaussian(seeds[6], (EXPERTS, FF, D), FF ** -0.5, 0.0625, ((0, 4), (1, 8)))
    grad_out = gaussian(seeds[7], (TOKENS, D), 0.25, 1.5, ((0, 8),))
    return dict(tokens=tokens, w_router=w_router, expert_ids=expert_ids, partner=partner, gate_weight=gate_weight, up_weight=up_weight, down_weight=down_weight, grad_out=grad_out)


exact_mode = lax.Precision.HIGHEST


def rounded(values):
    return lax.optimization_barrier(values.astype(jnp.bfloat16)).astype(jnp.float32)


def expert_pass(bundle):
    rows_in, cot_in, w_gate, w_up, w_down = bundle
    pre_gate = jnp.dot(rows_in, w_gate, preferred_element_type=jnp.float32)
    pre_up = jnp.dot(rows_in, w_up, preferred_element_type=jnp.float32)
    sigmoid_gate = jax.nn.sigmoid(pre_gate)
    swished = pre_gate * sigmoid_gate
    hidden = (swished * pre_up).astype(jnp.bfloat16)
    dhidden = jnp.dot(cot_in, w_down.T, preferred_element_type=jnp.float32)
    up_grad = (dhidden * swished).astype(jnp.bfloat16)
    gate_grad = (dhidden * pre_up * sigmoid_gate * (1.0 + pre_gate * (1.0 - sigmoid_gate))).astype(jnp.bfloat16)
    part_width = FF // (N_DP * N_MP)
    expert_out = jnp.zeros((rows_in.shape[0], D), jnp.float32)
    row_grads = jnp.zeros((rows_in.shape[0], D), jnp.float32)
    for segment in range(N_DP * N_MP):
        first_col = segment * part_width
        last_col = first_col + part_width
        product = jnp.dot(hidden[:, first_col:last_col], w_down[first_col:last_col], preferred_element_type=jnp.float32)
        expert_out = expert_out + rounded(product)
        backward = jnp.dot(gate_grad[:, first_col:last_col], w_gate[:, first_col:last_col].T, preferred_element_type=jnp.float32)
        backward = backward + jnp.dot(up_grad[:, first_col:last_col], w_up[:, first_col:last_col].T, preferred_element_type=jnp.float32)
        row_grads = row_grads + rounded(backward)
    grad_down = jnp.dot(hidden.T, cot_in, preferred_element_type=jnp.float32).astype(jnp.bfloat16)
    grad_gate = jnp.dot(rows_in.T, gate_grad, preferred_element_type=jnp.float32).astype(jnp.bfloat16)
    grad_up = jnp.dot(rows_in.T, up_grad, preferred_element_type=jnp.float32).astype(jnp.bfloat16)
    return expert_out.astype(jnp.bfloat16), row_grads.astype(jnp.bfloat16), grad_gate, grad_up, grad_down


def reference(tokens, w_router, expert_ids, partner, gate_weight, up_weight, down_weight, grad_out):
    blocks = TOKENS // TOK_DEV
    floats = tokens.astype(jnp.float32)
    logits = jnp.dot(floats, w_router, precision=exact_mode)
    chosen = (expert_ids[:, :, None] == jnp.arange(EXPERTS, dtype=jnp.int32)[None, None, :]).astype(jnp.int32)
    chosen_float = chosen.astype(jnp.float32)
    picked = jnp.sum(logits[:, None, :] * chosen_float, axis=2)
    share_one = jax.nn.sigmoid(picked[:, 0] - picked[:, 1])
    shares = jnp.stack([share_one, 1.0 - share_one], axis=1)
    grouped = chosen.reshape(blocks, 2 * TOK_DEV, EXPERTS)
    earlier = jnp.cumsum(grouped, axis=1) - grouped
    arrival = jnp.sum(earlier * grouped, axis=2).reshape(TOKENS, 2).astype(jnp.int32)
    partner_of = jnp.sum(chosen * partner[None, None, :], axis=2).astype(jnp.int32)
    target = jnp.where(arrival < CAP, expert_ids, partner_of).astype(jnp.int32)
    block_of = (jnp.arange(TOKENS, dtype=jnp.int32) // TOK_DEV)[:, None]
    slot_index = ((target * blocks + block_of) * MOST + arrival).reshape(-1).astype(jnp.int32)
    total_slots = EXPERTS * blocks * MOST
    per_expert = blocks * MOST
    copies = jnp.broadcast_to(tokens[:, None, :], (TOKENS, 2, D)).reshape(-1, D)
    expert_rows = jnp.zeros((total_slots, D), jnp.bfloat16).at[slot_index].set(copies)
    scaled = (shares[:, :, None] * grad_out.astype(jnp.float32)[:, None, :]).astype(jnp.bfloat16).reshape(-1, D)
    cot_rows = jnp.zeros((total_slots, D), jnp.bfloat16).at[slot_index].set(scaled)
    results = lax.map(expert_pass, (expert_rows.reshape(EXPERTS, per_expert, D), cot_rows.reshape(EXPERTS, per_expert, D), gate_weight, up_weight, down_weight))
    expert_out, row_grads, grad_gate, grad_up, grad_down = results
    back_rows = expert_out.reshape(total_slots, D)[slot_index].astype(jnp.float32).reshape(TOKENS, 2, D)
    mixed = (shares[:, 0, None] * back_rows[:, 0] + shares[:, 1, None] * back_rows[:, 1]).astype(jnp.bfloat16)
    falling = grad_out.astype(jnp.float32)
    dshare = jnp.sum(falling[:, None, :] * back_rows, axis=2)
    dlogit = shares[:, 0] * shares[:, 1] * (dshare[:, 0] - dshare[:, 1])
    grad_logits = (chosen_float[:, 0] - chosen_float[:, 1]) * dlogit[:, None]
    grad_router = jnp.dot(floats.T, grad_logits, precision=exact_mode)
    router_back = jnp.dot(grad_logits, w_router.T, precision=exact_mode)
    grad_rows = row_grads.reshape(total_slots, D)[slot_index].astype(jnp.float32).reshape(TOKENS, 2, D)
    grad_tokens = (router_back + grad_rows[:, 0] + grad_rows[:, 1]).astype(jnp.bfloat16)
    return (mixed, grad_tokens, grad_router, grad_gate, grad_up, grad_down)
```

```python
import jax
import jax.numpy as jnp
from jax import lax
from jax.sharding import PartitionSpec as P


def split3(values):
    high = values.astype(jnp.bfloat16)
    rest = values - high.astype(jnp.float32)
    middle = rest.astype(jnp.bfloat16)
    low = (rest - middle.astype(jnp.float32)).astype(jnp.bfloat16)
    return high, middle, low


def routing(tokens, w_router, expert_ids, partner):
    tok_rows = tokens.shape[0]
    experts = w_router.shape[1]
    slot_count = min(tok_rows, 4 * tok_rows // experts)
    keep_count = 3 * slot_count // 4
    pieces = jnp.concatenate(split3(w_router), axis=1)
    logits = jnp.dot(tokens, pieces, preferred_element_type=jnp.float32)
    logits = logits.reshape(tok_rows, 3, experts)
    logits = (logits[:, 2] + logits[:, 1]) + logits[:, 0]
    columns = lax.broadcasted_iota(jnp.int32, (tok_rows, experts), 1)
    first = expert_ids[:, :1] == columns
    second = expert_ids[:, 1:] == columns
    first_float = first.astype(jnp.float32)
    second_float = second.astype(jnp.float32)
    difference = jnp.sum(logits * (first_float - second_float), axis=1, keepdims=True)
    share_one = jax.nn.sigmoid(difference)
    share_two = 1.0 - share_one
    rows = lax.broadcasted_iota(jnp.int32, (tok_rows, tok_rows), 0)
    before = (lax.broadcasted_iota(jnp.int32, (tok_rows, tok_rows), 1) < rows).astype(jnp.bfloat16)
    named = (first_float + second_float).astype(jnp.bfloat16)
    earlier = jnp.dot(before, named, preferred_element_type=jnp.float32)
    arrival_one = jnp.sum(earlier * first_float, axis=1, keepdims=True)
    arrival_two = jnp.sum(earlier * second_float, axis=1, keepdims=True)
    mate = partner[None, :]
    mate_one = jnp.sum(jnp.where(first, mate, 0), axis=1, keepdims=True)
    mate_two = jnp.sum(jnp.where(second, mate, 0), axis=1, keepdims=True)
    target_one = jnp.where(arrival_one < keep_count, expert_ids[:, :1], mate_one)
    target_two = jnp.where(arrival_two < keep_count, expert_ids[:, 1:], mate_two)
    lands_one = (target_one == columns).astype(jnp.float32)
    lands_two = (target_two == columns).astype(jnp.float32)
    weight = share_one * lands_one + share_two * lands_two
    slope = share_one * share_two * (lands_one - lands_two)
    return weight, slope, first_float - second_float


def swap(values, axis, flip):
    size = lax.axis_size(axis)
    return lax.ppermute(values, axis, [(place, place ^ flip) for place in range(size)])


def bits(axis):
    return [1 << bit for bit in range(lax.axis_size(axis).bit_length() - 1)]


def few():
    return lax.axis_size("dp") * lax.axis_size("expert") <= 8


def own_place():
    if few():
        return 0
    return lax.axis_index("dp") * lax.axis_size("expert") + lax.axis_index("expert")


def spread(block):
    if not few():
        return [lax.all_gather(block, ("dp", "expert"), axis=0, tiled=True)]
    if lax.axis_size("expert") == 4:
        half = block.shape[1] // 2
        beside = swap(block, "expert", 1)
        above = swap(block, "expert", 2)
        across = jnp.concatenate(
            [swap(above[:, :half], "expert", 1), swap(beside[:, half:], "expert", 2)], axis=1
        )
        found = [block, beside, above, across]
    else:
        found = [block]
        for flip in bits("expert"):
            found = found + [swap(item, "expert", flip) for item in found]
    for flip in bits("dp"):
        found = found + [swap(item, "dp", flip) for item in found]
    return found


def spread_small(block):
    if not few():
        return lax.all_gather(block, ("dp", "expert"), axis=0, tiled=False)
    found = block[None]
    for axis in ("expert", "dp"):
        for flip in bits(axis):
            found = jnp.concatenate([found, swap(found, axis, flip)], axis=0)
    return found


def total(values):
    if not few():
        return lax.psum(values, ("dp", "expert", "mp"))
    experts = lax.axis_size("expert")
    for axis, scale in (("expert", 1), ("dp", experts), ("mp", 0)):
        for flip in bits(axis):
            arrived = swap(values, axis, flip)
            if scale:
                arrived = arrived.reshape(-1, 2, flip * scale, values.shape[1])
                arrived = jnp.flip(arrived, axis=1).reshape(values.shape)
            values = values + arrived
    return values


def sum_over_mp(values):
    if lax.axis_size("mp") == 1:
        return values.astype(jnp.bfloat16)
    half = values.shape[1] // 2
    odd = (lax.axis_index("mp") & 1) == 1
    left, right = values[:, :half], values[:, half:]
    kept = jnp.where(odd, right, left) + swap(
        jnp.where(odd, left, right).astype(jnp.bfloat16), "mp", 1
    ).astype(jnp.float32)
    kept = kept.astype(jnp.bfloat16)
    for flip in bits("mp")[1:]:
        kept = (kept.astype(jnp.float32) + swap(kept, "mp", flip).astype(jnp.float32)).astype(
            jnp.bfloat16
        )
    other = swap(kept, "mp", 1)
    return jnp.concatenate([jnp.where(odd, other, kept), jnp.where(odd, kept, other)], axis=1)


def collect(partial_value, tok_rows):
    if not few():
        own = lax.psum_scatter(
            partial_value.astype(jnp.bfloat16), ("dp", "expert"), scatter_dimension=0, tiled=True
        )
        return lax.psum(own, "mp")
    features = partial_value.shape[1]
    parts = partial_value.reshape(-1, tok_rows, features)
    blocks = lax.axis_size("expert")
    for flip in reversed(bits("dp")):
        grouped = parts.reshape(2, -1, tok_rows, features)
        parts = grouped[0] + swap(grouped[1].astype(jnp.bfloat16), "dp", flip).astype(jnp.float32)
    ways = bits("expert")
    width = features // len(ways)
    sums = []
    for turn in range(len(ways)):
        piece = parts[:, :, turn * width : (turn + 1) * width]
        done = []
        left = list(range(blocks))
        held = {place: piece[place] for place in left}
        for flip in ways[turn:] + ways[:turn]:
            sent = [place for place in held if place & flip]
            arrived = swap(
                jnp.stack([held[place] for place in sent]).astype(jnp.bfloat16), "expert", flip
            ).astype(jnp.float32)
            for number, place in enumerate(sent):
                held[place ^ flip] = held[place ^ flip] + arrived[number]
                del held[place]
        sums.append(sum_over_mp(held[0]))
    return jnp.concatenate(sums, axis=1)


def local(tokens, w_router, expert_ids, partner, gate_weight, up_weight, down_weight, grad_out):
    tok_rows = tokens.shape[0]
    experts = w_router.shape[1]
    all_tokens = jnp.concatenate(spread(tokens), axis=0)
    all_grads = jnp.concatenate(spread(grad_out), axis=0)
    weight, slope, sign = routing(tokens, w_router, expert_ids, partner)
    small = spread_small(jnp.concatenate([weight, slope, sign], axis=1))
    blocks = small.shape[0]
    small = small.reshape(blocks * tok_rows, 3 * experts)
    mine = (lax.iota(jnp.int32, experts) == lax.axis_index("expert")).astype(jnp.float32)
    weight_all = jnp.sum(small[:, :experts] * mine, axis=1, keepdims=True)
    slope_all = jnp.sum(small[:, experts : 2 * experts] * mine, axis=1)
    sign_all = small[:, 2 * experts :]

    w_gate = gate_weight[0]
    w_up = up_weight[0]
    w_down = down_weight[0]
    pre_gate = jnp.dot(all_tokens, w_gate, preferred_element_type=jnp.float32)
    pre_up = jnp.dot(all_tokens, w_up, preferred_element_type=jnp.float32)
    sigmoid_gate = jax.nn.sigmoid(pre_gate)
    swished = pre_gate * sigmoid_gate
    product = swished * pre_up
    hidden = (weight_all * product).astype(jnp.bfloat16)
    mixed = collect(jnp.dot(hidden, w_down, preferred_element_type=jnp.float32), tok_rows)

    back = jnp.einsum("rd,fd->rf", all_grads, w_down, preferred_element_type=jnp.float32)
    dshare = jnp.sum(product * back, axis=1)
    dhidden = weight_all * back
    up_grad = (dhidden * swished).astype(jnp.bfloat16)
    gate_grad = (dhidden * pre_up * sigmoid_gate * (1.0 + pre_gate * (1.0 - sigmoid_gate))).astype(
        jnp.bfloat16
    )
    dlogit = total((slope_all * dshare).reshape(blocks, tok_rows))
    row_grads = collect(
        jnp.einsum("rf,df->rd", gate_grad, w_gate, preferred_element_type=jnp.float32)
        + jnp.einsum("rf,df->rd", up_grad, w_up, preferred_element_type=jnp.float32),
        tok_rows,
    )
    grad_down = jnp.einsum("rf,rd->fd", hidden, all_grads, preferred_element_type=jnp.float32)
    grad_gate = jnp.einsum("rd,rf->df", all_tokens, gate_grad, preferred_element_type=jnp.float32)
    grad_up = jnp.einsum("rd,rf->df", all_tokens, up_grad, preferred_element_type=jnp.float32)

    grad_logits = sign_all * dlogit.reshape(-1, 1)
    pieces = jnp.concatenate(split3(grad_logits), axis=1)
    grad_router = jnp.einsum("rd,re->de", all_tokens, pieces, preferred_element_type=jnp.float32)
    grad_router = (
        grad_router[:, 2 * experts :] + grad_router[:, experts : 2 * experts]
    ) + grad_router[:, :experts]
    own_logits = lax.dynamic_slice_in_dim(grad_logits, own_place() * tok_rows, tok_rows, 0)
    router_back = jnp.dot(own_logits, w_router.T, precision=lax.Precision.HIGHEST)
    grad_tokens = (router_back + row_grads.astype(jnp.float32)).astype(jnp.bfloat16)
    return (
        mixed,
        grad_tokens,
        grad_router,
        grad_gate.astype(jnp.bfloat16)[None],
        grad_up.astype(jnp.bfloat16)[None],
        grad_down.astype(jnp.bfloat16)[None],
    )


def solution(mesh):
    in_specs = (
        P(("dp", "expert"), None),
        P(),
        P(("dp", "expert"), None),
        P(),
        P("expert", None, ("dp", "mp")),
        P("expert", None, ("dp", "mp")),
        P("expert", ("dp", "mp"), None),
        P(("dp", "expert"), None),
    )
    out_specs = (
        P(("dp", "expert"), None),
        P(("dp", "expert"), None),
        P(),
        P("expert", None, ("dp", "mp")),
        P("expert", None, ("dp", "mp")),
        P("expert", ("dp", "mp"), None),
    )
    return jax.shard_map(local, mesh=mesh, in_specs=in_specs, out_specs=out_specs, check_vma=False)
```

```python
import functools

import jax
import jax.numpy as jnp
from jax import lax
from jax.experimental import pallas as pl
from jax.experimental.pallas import tpu as pltpu
from jax.sharding import PartitionSpec as P


def split3(values):
    high = values.astype(jnp.bfloat16)
    rest = values - high.astype(jnp.float32)
    middle = rest.astype(jnp.bfloat16)
    low = (rest - middle.astype(jnp.float32)).astype(jnp.bfloat16)
    return high, middle, low


def routing(tokens, w_router, expert_ids, partner):
    tok_rows = tokens.shape[0]
    experts = w_router.shape[1]
    slot_count = min(tok_rows, 4 * tok_rows // experts)
    keep_count = 3 * slot_count // 4
    pieces = jnp.concatenate(split3(w_router), axis=1)
    logits = jnp.dot(tokens, pieces, preferred_element_type=jnp.float32)
    logits = logits.reshape(tok_rows, 3, experts)
    logits = (logits[:, 2] + logits[:, 1]) + logits[:, 0]
    columns = lax.broadcasted_iota(jnp.int32, (tok_rows, experts), 1)
    first = expert_ids[:, :1] == columns
    second = expert_ids[:, 1:] == columns
    first_float = first.astype(jnp.float32)
    second_float = second.astype(jnp.float32)
    difference = jnp.sum(logits * (first_float - second_float), axis=1, keepdims=True)
    share_one = jax.nn.sigmoid(difference)
    share_two = 1.0 - share_one
    rows = lax.broadcasted_iota(jnp.int32, (tok_rows, tok_rows), 0)
    before = (lax.broadcasted_iota(jnp.int32, (tok_rows, tok_rows), 1) < rows).astype(jnp.bfloat16)
    named = (first_float + second_float).astype(jnp.bfloat16)
    earlier = jnp.dot(before, named, preferred_element_type=jnp.float32)
    arrival_one = jnp.sum(earlier * first_float, axis=1, keepdims=True)
    arrival_two = jnp.sum(earlier * second_float, axis=1, keepdims=True)
    mate = partner[None, :]
    mate_one = jnp.sum(jnp.where(first, mate, 0), axis=1, keepdims=True)
    mate_two = jnp.sum(jnp.where(second, mate, 0), axis=1, keepdims=True)
    target_one = jnp.where(arrival_one < keep_count, expert_ids[:, :1], mate_one)
    target_two = jnp.where(arrival_two < keep_count, expert_ids[:, 1:], mate_two)
    lands_one = (target_one == columns).astype(jnp.float32)
    lands_two = (target_two == columns).astype(jnp.float32)
    weight = share_one * lands_one + share_two * lands_two
    slope = share_one * share_two * (lands_one - lands_two)
    return weight, slope, first_float - second_float


def swap(values, axis, flip):
    size = lax.axis_size(axis)
    return lax.ppermute(values, axis, [(place, place ^ flip) for place in range(size)])


NT = (((1,), (1,)), ((), ()))
TN = (((0,), (0,)), ((), ()))
WHOLE = pl.BlockSpec(memory_space=pltpu.VMEM)
LEFT = pl.BlockSpec(memory_space=pl.ANY)


def settings():
    return pltpu.CompilerParams(vmem_limit_bytes=40 << 20)


def after(values, pins):
    if not pins:
        return values
    return lax.optimization_barrier((values, *pins))[0]


def on_hbm(*arrays):
    return tuple(pltpu.with_memory_space_constraint(array, pltpu.HBM) for array in arrays)


def in_hbm(shape, dtype=jnp.bfloat16):
    return pltpu.HBM(shape, dtype)


def in_vmem(shape, dtype=jnp.bfloat16):
    return pltpu.VMEM(shape, dtype)


def cost(flops, moved):
    return pl.CostEstimate(flops=flops, bytes_accessed=moved, transcendentals=0)


def once(shape):
    return pl.BlockSpec(shape, lambda i: (0,) * len(shape), pipeline_mode=pl.Buffered(1))


def shaped(shape, dtype=jnp.bfloat16):
    return jax.ShapeDtypeStruct(shape, dtype)


def routing_kernel(experts, keep_count, tokens, w_router, ids, partner, out):
    tok_rows = tokens.shape[0]
    high, middle, low = split3(w_router[...])

    def product(piece):
        return lax.dot_general(piece, tokens[...], NT, preferred_element_type=jnp.float32)

    logits = (product(low) + product(middle)) + product(high)
    names = lax.broadcasted_iota(jnp.int32, (experts, tok_rows), 0)
    first = (ids[0:1, :] == names).astype(jnp.float32)
    second = (ids[1:2, :] == names).astype(jnp.float32)
    difference = jnp.sum(logits * (first - second), axis=0, keepdims=True)
    share_one = jax.nn.sigmoid(difference)
    share_two = 1.0 - share_one
    source = lax.broadcasted_iota(jnp.int32, (tok_rows, tok_rows), 0)
    before = source < lax.broadcasted_iota(jnp.int32, (tok_rows, tok_rows), 1)
    earlier = jnp.dot(first + second, before.astype(jnp.float32), preferred_element_type=jnp.float32)
    arrival_one = jnp.sum(earlier * first, axis=0, keepdims=True)
    arrival_two = jnp.sum(earlier * second, axis=0, keepdims=True)
    mates = jnp.zeros(names.shape, jnp.int32)
    for expert in range(experts):
        mates = jnp.where(names == expert, partner[expert], mates)
    mates = mates.astype(jnp.float32)
    place = names.astype(jnp.float32)

    def lands(chosen, arrival):
        own = jnp.sum(chosen * place, axis=0, keepdims=True)
        mate = jnp.sum(chosen * mates, axis=0, keepdims=True)
        target = jnp.where(arrival < keep_count, own, mate)
        return (target == place).astype(jnp.float32)

    lands_one = lands(first, arrival_one)
    lands_two = lands(second, arrival_two)
    out[0:experts, :] = share_one * lands_one + share_two * lands_two
    out[experts : 2 * experts, :] = share_one * share_two * (lands_one - lands_two)
    out[2 * experts :, :] = first - second


def route(tokens, w_router, expert_ids, partner):
    tok_rows = tokens.shape[0]
    experts = w_router.shape[1]
    slot_count = min(tok_rows, 4 * tok_rows // experts)
    return pl.pallas_call(
        functools.partial(routing_kernel, experts, 3 * slot_count // 4),
        out_shape=shaped((3 * experts, tok_rows), jnp.float32),
        in_specs=[WHOLE] * 3 + [pl.BlockSpec(memory_space=pltpu.SMEM)],
        out_specs=WHOLE,
        name="route",
        cost_estimate=cost(1 << 20, 1 << 20),
    )(tokens, w_router.T, expert_ids.T, partner)


def tile_of(number, size):
    return pl.ds(pl.multiple_of(number * size, size), size)


class Mover:
    def __init__(self, sems):
        self.sems = sems
        self.used = 0

    def start(self, source, target):
        copy = pltpu.make_async_copy(source, target, self.sems.at[self.used])
        self.used += 1
        copy.start()
        return copy


def fetch_rows(mover, blocks, rows):
    count = blocks[0].shape[0]
    return [
        mover.start(block, rows.at[pl.ds(number * count, count), :])
        for number, block in enumerate(blocks)
    ]


def forward(blocks, w_gate, w_up, tile):
    number = len(blocks)
    tok_rows, features = blocks[0].shape
    count = number * tok_rows
    width = w_gate.shape[1]

    def body(*refs):
        pieces, refs = refs[:number], refs[number:]
        wg, wu, hid, sw, sg, everything, x, bg, bu, gates, h, a, b, sems_in, sems_out = refs
        mover, outward = Mover(sems_in), Mover(sems_out)
        copies = [mover.start(wg, bg)]
        for copy in fetch_rows(mover, pieces, x):
            copy.wait()
        copies.append(mover.start(wu, bu))
        copies[0].wait()
        tiles = [pl.ds(step * tile, tile) for step in range(width // tile)]
        for place in tiles:
            gates[:, place] = jnp.dot(x[...], bg[:, place], preferred_element_type=jnp.float32)
        done = [outward.start(x, everything)]
        copies[1].wait()
        for place in tiles:
            up = jnp.dot(x[...], bu[:, place], preferred_element_type=jnp.float32)
            gate = gates[:, place]
            sigmoid_gate = jax.nn.sigmoid(gate)
            swished = gate * sigmoid_gate
            h[:, place] = (swished * up).astype(jnp.bfloat16)
            a[:, place] = swished.astype(jnp.bfloat16)
            b[:, place] = (up * sigmoid_gate * (1.0 + gate * (1.0 - sigmoid_gate))).astype(
                jnp.bfloat16
            )
        done += [outward.start(h, hid), outward.start(a, sw), outward.start(b, sg)]
        for copy in done:
            copy.wait()

    flat = pltpu.VMEM((count, width), jnp.bfloat16)
    weights = pltpu.VMEM((features, width), jnp.bfloat16)
    return pl.pallas_call(
        body,
        out_shape=(in_hbm((count, width)),) * 3 + (in_hbm((count, features)),),
        in_specs=[LEFT] * (number + 2),
        out_specs=(LEFT,) * 4,
        scratch_shapes=[
            pltpu.VMEM((count, features), jnp.bfloat16),
            weights,
            weights,
            pltpu.VMEM((count, width), jnp.float32),
            flat,
            flat,
            flat,
            pltpu.SemaphoreType.DMA((number + 2,)),
            pltpu.SemaphoreType.DMA((4,)),
        ],
        compiler_params=pltpu.CompilerParams(vmem_limit_bytes=40 << 20),
        name="forward",
        cost_estimate=cost(4 * count * features * width, 6 * features * width),
    )(*on_hbm(*blocks, w_gate, w_up))


def down(core, hidden, w_down, tile, pins):
    count, width = hidden.shape
    half = w_down.shape[1] // 2
    steps = half // tile
    hidden = after(hidden, pins)

    def body(core_ref, hid, wd, keep, send, h, bd, k, s, sems_in, sems_out):
        mover, outward = Mover(sems_in), Mover(sems_out)
        copies = [mover.start(hid, h), mover.start(wd, bd)]
        for copy in copies:
            copy.wait()
        me = core_ref[0]
        done = []
        for side, target, out in ((1 - me, s, send), (me, k, keep)):
            for step in range(steps):
                source = pl.ds(pl.multiple_of(side * half + step * tile, tile), tile)
                columns = pl.ds(step * tile, tile)
                target[:, columns] = jnp.dot(
                    h[...], bd[:, source], preferred_element_type=jnp.float32
                ).astype(jnp.bfloat16)
                done.append(outward.start(target.at[:, columns], out.at[:, columns]))
        for copy in done:
            copy.wait()

    part = pltpu.VMEM((count, half), jnp.bfloat16)
    return pl.pallas_call(
        body,
        out_shape=(in_hbm((count, half)),) * 2,
        in_specs=[pl.BlockSpec(memory_space=pltpu.SMEM)] + [LEFT] * 2,
        out_specs=(LEFT,) * 2,
        scratch_shapes=[
            pltpu.VMEM((count, width), jnp.bfloat16),
            pltpu.VMEM((width, 2 * half), jnp.bfloat16),
            part,
            part,
            pltpu.SemaphoreType.DMA((2,)),
            pltpu.SemaphoreType.DMA((2 * steps,)),
        ],
        compiler_params=pltpu.CompilerParams(vmem_limit_bytes=24 << 20),
        name="down",
        cost_estimate=cost(4 * count * half * width, 4 * half * width),
    )(core, *on_hbm(hidden, w_down))


def backward(blocks, w_down, hidden, sw, sg, weight, slope, tile):
    number = len(blocks)
    tok_rows, features = blocks[0].shape
    count = number * tok_rows
    width = w_down.shape[0]

    def body(*refs):
        pieces, refs = refs[:number], refs[number:]
        wd, hid, swished, slopes, c, v, up_out, gate_out, hidden_out, ds, everything = refs[:11]
        x, bd, h, a, b, ug, gg, hc, sems_in, sems_out = refs[11:]
        mover, outward = Mover(sems_in), Mover(sems_out)
        moves = fetch_rows(mover, pieces, x)
        tiles = [pl.ds(step * tile, tile) for step in range(width // tile)]
        copies = [mover.start(wd.at[tiles[0], :], bd.at[tiles[0], :])]
        for copy in moves:
            copy.wait()
        rest = [mover.start(hid, h), mover.start(swished, a), mover.start(slopes, b)]
        ds[...] = jnp.zeros_like(ds)
        scale = c[...]
        for step, place in enumerate(tiles):
            if step + 1 < len(tiles):
                following = tiles[step + 1]
                copies.append(mover.start(wd.at[following, :], bd.at[following, :]))
            copies[step].wait()
            if step == 0:
                done = [outward.start(x, everything)]
            back = lax.dot_general(x[...], bd[place, :], NT, preferred_element_type=jnp.float32)
            if step == 0:
                for copy in rest:
                    copy.wait()
            value = h[:, place].astype(jnp.float32)
            ds[...] += jnp.sum(value * back, axis=1, keepdims=True) * v[...]
            hc[:, place] = (value * scale).astype(jnp.bfloat16)
            back = back * scale
            ug[:, place] = (back * a[:, place].astype(jnp.float32)).astype(jnp.bfloat16)
            gg[:, place] = (back * b[:, place].astype(jnp.float32)).astype(jnp.bfloat16)
        done += [
            outward.start(ug, up_out),
            outward.start(gg, gate_out),
            outward.start(hc, hidden_out),
        ]
        for copy in done:
            copy.wait()

    flat = pltpu.VMEM((count, width), jnp.bfloat16)
    return pl.pallas_call(
        body,
        out_shape=(in_hbm((count, width)),) * 3
        + (shaped((count, 1), jnp.float32), in_hbm((count, features))),
        in_specs=[LEFT] * (number + 4) + [WHOLE] * 2,
        out_specs=(LEFT,) * 3 + (WHOLE, LEFT),
        scratch_shapes=[
            pltpu.VMEM((count, features), jnp.bfloat16),
            pltpu.VMEM((width, features), jnp.bfloat16),
        ]
        + [flat] * 6
        + [
            pltpu.SemaphoreType.DMA((number + width // tile + 3,)),
            pltpu.SemaphoreType.DMA((4,)),
        ],
        compiler_params=pltpu.CompilerParams(vmem_limit_bytes=40 << 20),
        name="backward",
        cost_estimate=cost(2 * count * features * width, 2 * features * width),
    )(*on_hbm(*blocks, w_down, hidden, sw, sg), weight, slope)


def rows_back(core, gate_grad, up_grad, w_gate, w_up, first, last, tile, pins):
    count, width = gate_grad.shape
    half = w_gate.shape[0] // 2
    gate_grad = after(gate_grad, pins)
    steps = (last - first) // tile

    def body(core_ref, gate_in, up_in, wg, wu, keep, send, gg, ug, bg, bu, k, s, sems_in, sems_out):
        mover, outward = Mover(sems_in), Mover(sems_out)
        me = core_ref[0]
        pieces = []
        for side, target, out in ((1 - me, s, send), (me, k, keep)):
            for step in range(steps):
                source = pl.ds(pl.multiple_of(side * half + first + step * tile, tile), tile)
                pieces.append((source, target, pl.ds(step * tile, tile), out))
        copies = []

        def load(number):
            if number < len(pieces):
                source, place = pieces[number][0], pl.ds(number * tile, tile)
                copies.append(mover.start(wg.at[source, :], bg.at[place, :]))
                copies.append(mover.start(wu.at[source, :], bu.at[place, :]))

        rows = [mover.start(gate_in, gg), mover.start(up_in, ug)]
        load(0)
        for copy in rows:
            copy.wait()
        done = []
        for number, (_, target, columns, out) in enumerate(pieces):
            load(number + 1)
            place = pl.ds(number * tile, tile)
            copies[2 * number].wait()
            total = lax.dot_general(gg[...], bg[place, :], NT, preferred_element_type=jnp.float32)
            copies[2 * number + 1].wait()
            total = total + lax.dot_general(
                ug[...], bu[place, :], NT, preferred_element_type=jnp.float32
            )
            target[:, columns] = total.astype(jnp.bfloat16)
            done.append(outward.start(target.at[:, columns], out.at[:, columns]))
        for copy in done:
            copy.wait()

    flat = pltpu.VMEM((count, width), jnp.bfloat16)
    weights = pltpu.VMEM((2 * (last - first), width), jnp.bfloat16)
    part = pltpu.VMEM((count, last - first), jnp.bfloat16)
    return pl.pallas_call(
        body,
        out_shape=(in_hbm((count, last - first)),) * 2,
        in_specs=[pl.BlockSpec(memory_space=pltpu.SMEM)] + [LEFT] * 4,
        out_specs=(LEFT,) * 2,
        scratch_shapes=[flat, flat, weights, weights, part, part]
        + [pltpu.SemaphoreType.DMA((4 * steps + 2,)), pltpu.SemaphoreType.DMA((2 * steps,))],
        compiler_params=pltpu.CompilerParams(vmem_limit_bytes=40 << 20),
        name="rows_back",
        cost_estimate=cost(8 * count * (last - first) * width, 8 * (last - first) * width),
    )(core, *on_hbm(gate_grad, up_grad, w_gate, w_up))


def outer(left, right, pins):
    left = after(left, pins)
    return lax.dot_general(left, right, TN, preferred_element_type=jnp.float32).astype(jnp.bfloat16)


def small_call(body, outs, args, pins, name):
    first = after(args[0], pins)
    return pl.pallas_call(
        body,
        out_shape=tuple(outs),
        in_specs=[WHOLE] * len(args),
        out_specs=(WHOLE,) * len(outs),
        compiler_params=settings(),
        name=name,
        cost_estimate=cost(1 << 20, 1 << 20),
    )(first, *args[1:])


def add(one, two):
    return (one.astype(jnp.float32) + two.astype(jnp.float32)).astype(jnp.bfloat16)


def trade(values, kind):
    cores, experts = lax.axis_size("dp"), lax.axis_size("expert")
    pairs = []
    for core in range(cores):
        for place in range(experts):
            flip = {"peer": 0, "first": 1 + core, "second": 2 - core, "both": 3}[kind]
            other = core ^ 1 if kind == "peer" else core
            pairs.append((core * experts + place, other * experts + (place ^ flip)))
    return lax.ppermute(values, ("dp", "expert"), pairs)


TAIL = 16


def pack(values):
    high, middle, low = split3(values)
    shape = (TAIL, values.shape[1])
    row = lax.broadcasted_iota(jnp.int32, shape, 0)
    out = jnp.zeros(shape, jnp.float32)
    for number, piece in enumerate((high, middle, low)):
        out = jnp.where(row == number, piece.astype(jnp.float32), out)
    return out.astype(jnp.bfloat16)


def unpack(block):
    return jnp.sum(block.astype(jnp.float32), axis=0, keepdims=True)


class Reduction:
    def __init__(self, keep, send, tok_rows, odd, rider=None):
        self.rows = tok_rows
        self.width = keep.shape[1]
        self.keep = (keep,)
        self.odd = odd
        self.rider = rider
        self.arrived = (trade(send, "peer"),)

    def spread_part(self, number, pins):
        rows = self.rows

        def body(inputs, sent, kept):
            keep, arrived = inputs
            for side in range(2):
                for place, there in enumerate((0, 2, 1, 3)):
                    away = place in ((1, 3), (2, 3))[number]
                    slot = 2 * side + (place // 2, place % 2)[number]
                    (sent if away else kept)[0][pl.ds(slot * rows, rows), :] = add(
                        keep[pl.ds((4 * side + place) * rows, rows), :],
                        arrived[pl.ds((4 * (1 - side) + there) * rows, rows), :],
                    )

        shape = (4 * rows, self.width)
        sent = self.run(body, [shape], [shape], [], pins, "spread_part", False)
        self.arrived = (trade(sent[0], ("first", "second")[number]),)
        return list(self.keep)

    def cross_part(self, number, pins):
        rows = self.rows

        def body(inputs, sent, kept):
            keep, arrived = inputs
            for place in range(4):
                out = (sent if place % 2 else kept)[0]
                source = pl.ds(place * rows, rows)
                out[pl.ds(place // 2 * rows, rows), :] = add(keep[source, :], arrived[source, :])

        shape = (2 * rows, self.width)
        sent = self.run(body, [shape], [shape], [], pins, "cross_part", True)
        self.arrived = (trade(sent[0], ("second", "first")[number]),)
        return list(self.keep)

    def halve_part(self, pins):
        rows, half = 2 * self.rows, self.width // 2

        def body(inputs, sent, kept):
            one = add(inputs[0][:, :half], inputs[1][:, :half])
            two = add(inputs[0][:, half:], inputs[1][:, half:])
            flag = inputs[2][...] > 0
            sent[0][...] = jnp.where(flag, one, two)
            kept[0][...] = jnp.where(flag, two, one)

        shape = (rows, half)
        sent = self.run(body, [shape], [shape], [self.odd], pins, "halve_part", True)
        self.arrived = (swap(sent[0], "mp", 1),)
        return list(self.keep)

    def run(self, body, sent, kept, extra, pins, name, rides):
        riding = self.rider is not None
        outs = [
            shaped((rows + (TAIL if riding and number == 0 else 0), width))
            for number, (rows, width) in enumerate(sent)
        ]
        outs += [shaped(shape) for shape in kept]
        args = [*self.keep, *self.arrived, *extra]
        tail_at = len(self.keep)
        if riding:
            args.append(self.rider)
            outs.append(shaped(self.rider.shape, jnp.float32))

        def whole(*refs):
            inputs, outputs = refs[: len(args)], refs[len(args) :]
            body(inputs, outputs[: len(sent)], outputs[len(sent) : len(sent) + len(kept)])
            if riding:
                total = inputs[-1][...]
                length = total.shape[1]
                if rides:
                    arrived = inputs[tail_at]
                    total = total + unpack(arrived[arrived.shape[0] - TAIL :, :length])
                outputs[-1][...] = total
                outputs[0][sent[0][0] :, :length] = pack(total)

        outs = small_call(whole, outs, args, pins, name)
        if riding:
            self.rider = outs[-1]
        self.keep = outs[len(sent) : len(sent) + len(kept)] if kept else (outs[0],)
        return outs[: len(sent)]

    def spread(self, pins, scale=None):
        rows, half = self.rows, self.width // 2

        def body(inputs, sent, kept):
            keep, arrived = inputs[0], inputs[1]
            for side in range(2):
                for place, there in enumerate((0, 2, 1, 3)):
                    source = pl.ds((4 * side + place) * rows, rows)
                    total = keep[source, :].astype(jnp.float32) + arrived[
                        pl.ds((4 * (1 - side) + there) * rows, rows), :
                    ].astype(jnp.float32)
                    if scale is not None:
                        total = total * inputs[2][source, :]
                    total = total.astype(jnp.bfloat16)
                    left = pl.ds((2 * side + place // 2) * rows, rows)
                    right = pl.ds((2 * side + place % 2) * rows, rows)
                    (sent if place in (1, 3) else kept)[0][left, :] = total[:, :half]
                    (sent if place in (2, 3) else kept)[1][right, :] = total[:, half:]

        extra = [] if scale is None else [scale]
        shape = (4 * rows, half)
        sent = self.run(body, [shape] * 2, [shape] * 2, extra, pins, "spread", False)
        self.arrived = (trade(sent[0], "first"), trade(sent[1], "second"))
        return list(self.keep[:1])

    def cross(self, pins):
        rows, half = self.rows, self.width // 2

        def body(inputs, sent, kept):
            for part in range(2):
                keep, arrived = inputs[part], inputs[2 + part]
                for place in range(4):
                    out = (sent if place % 2 else kept)[part]
                    source = pl.ds(place * rows, rows)
                    out[pl.ds(place // 2 * rows, rows), :] = add(
                        keep[source, :], arrived[source, :]
                    )

        shape = (2 * rows, half)
        sent = self.run(body, [shape] * 2, [shape] * 2, [], pins, "cross", True)
        self.arrived = (trade(sent[0], "second"), trade(sent[1], "first"))
        return list(self.keep[:1])

    def halve(self, pins):
        rows, half = 2 * self.rows, self.width // 2

        def body(inputs, sent, kept):
            one = add(inputs[0][...], inputs[2][:rows, :])
            two = add(inputs[1][...], inputs[3][...])
            flag = inputs[4][...] > 0
            sent[0][:rows, :] = jnp.where(flag, one, two)
            kept[0][...] = jnp.where(flag, two, one)

        shape = (rows, half)
        sent = self.run(body, [shape], [shape], [self.odd], pins, "halve", True)
        self.arrived = (swap(sent[0], "mp", 1),)
        return list(self.keep)

    def step(self, flip, pins):
        rows, half = 2 * self.rows, self.width // 2

        def body(inputs, sent, kept):
            sent[0][:rows, :] = add(inputs[0][:rows, :], inputs[1][:rows, :])

        sent = self.run(body, [(rows, half)], [], [], pins, "step", True)
        self.arrived = (swap(sent[0], "mp", flip),)
        return list(self.keep)

    def join(self, pins):
        rows, half = self.rows, self.width // 2

        def body(inputs, sent, kept):
            keep, arrived = inputs[0], inputs[1]
            flag = inputs[2][...] > 0
            for out, place in ((kept[0], pl.ds(0, rows)), (sent[0], pl.ds(rows, rows))):
                out[:rows, :half] = jnp.where(flag, arrived[place, :], keep[place, :])
                out[:rows, half:] = jnp.where(flag, keep[place, :], arrived[place, :])

        shape = (rows, self.width)
        sent = self.run(body, [shape], [shape], [self.odd], pins, "join", False)
        self.arrived = (trade(sent[0], "peer"),)
        return list(self.keep)


def finish(parts, core, extra, pins, name):
    rows, width = parts[0].keep[0].shape
    features = 2 * width * len(parts)
    rider = parts[0].rider
    riding = rider is not None
    args = [item for part in parts for item in (part.keep[0], part.arrived[0])]
    at = len(args)
    args += [core, *extra] + ([rider] if riding else [])
    outs = [shaped((rows, features))]
    if riding:
        outs.append(shaped(rider.shape, jnp.float32))

    def body(*refs):
        out = refs[len(args)]
        flag = refs[at][...] > 0
        for number in range(len(parts)):
            keep, arrived = refs[2 * number][...], refs[2 * number + 1][:rows, :]
            sides = (jnp.where(flag, arrived, keep), jnp.where(flag, keep, arrived))
            for side, values in enumerate(sides):
                columns = pl.ds(side * features // 2 + number * width, width)
                if extra:
                    values = values.astype(jnp.float32)
                    logits, router = refs[at + 1], refs[at + 2]
                    for expert in range(router.shape[0]):
                        values = values + logits[:, expert : expert + 1] * (
                            router[expert : expert + 1, columns]
                        )
                out[:, columns] = values.astype(jnp.bfloat16)
        if riding:
            own = refs[len(args) - 1][...]
            refs[-1][...] = own + unpack(refs[1][rows:, : own.shape[1]])

    return small_call(body, outs, args, pins, name)


def gather_rows(block, peer, near, second, far):
    near_peer, second_peer = trade(second, "peer"), trade(near, "peer")
    return [block, near, second, far, peer, near_peer, second_peer, trade(far, "peer")]


def swapped(blocks):
    return jnp.stack([blocks[0], blocks[2], blocks[1], blocks[3]])


def gather_small(small):
    found = jnp.stack([small, trade(small, "first")])
    return jnp.concatenate([found, trade(found, "second")], axis=0)


def order():
    core, expert = lax.axis_index("dp"), lax.axis_index("expert")
    flips = (0, 1 + core, 2 - core, 3)
    places = [(core ^ side) * 4 + (expert ^ flip) for side in range(2) for flip in flips]
    places = jnp.stack([jnp.asarray(place, jnp.int32) for place in places])
    return (lax.iota(jnp.int32, 8)[:, None] == places[None, :]).astype(jnp.float32)


def local_pairs(tokens, w_router, expert_ids, partner, gate_weight, up_weight, down_weight, grad_out):
    tok_rows, features = tokens.shape
    experts = w_router.shape[1]
    width = gate_weight.shape[2]
    w_gate, w_up, w_down = gate_weight[0], up_weight[0], down_weight[0]
    odd = (lax.axis_index("mp") & 1).astype(jnp.int32).reshape(1, 1)
    core = lax.axis_index("dp").astype(jnp.int32).reshape(1)

    tok_near = trade(tokens, "first")
    tok_second = trade(tokens, "second")
    tok_peer = trade(tokens, "peer")
    small = route(tokens, w_router, expert_ids, partner)
    tok_far = trade(after(tok_near, [small]), "second")
    small = gather_small(small)
    small_peer = trade(small, "peer")
    token_blocks = gather_rows(tokens, tok_peer, tok_near, tok_second, after(tok_far, [small]))
    later = after(grad_out, [tok_far])
    out_near = trade(later, "first")
    out_second = trade(later, "second")
    out_far = trade(later, "both")
    out_peer = trade(grad_out, "peer")
    hidden, sw, sg, all_tokens = forward(token_blocks, w_gate, w_up, width // 4)
    small = jnp.concatenate([small, swapped(after(small_peer, [hidden]))], axis=0)
    mine = (lax.iota(jnp.int32, experts) == lax.axis_index("expert")).astype(jnp.float32)
    mine = mine[None, :, None]
    weight = jnp.sum(small[:, :experts] * mine, axis=1).reshape(-1, 1)
    slope = jnp.sum(small[:, experts : 2 * experts] * mine, axis=1).reshape(-1, 1)
    keep, send = down(core, hidden, w_down, features // 4, [])
    out_near, out_second, out_far = (
        after(item, [keep]) for item in (out_near, out_second, out_far)
    )
    grad_blocks = gather_rows(grad_out, out_peer, out_near, out_second, out_far)
    send = after(send, [out_near, out_second, out_far])
    mixed = Reduction(keep, send, tok_rows, odd)
    up_grad, gate_grad, hidden, dshare, all_grads = backward(
        grad_blocks, w_down, hidden, sw, sg, weight, slope, width // 2
    )
    places = order()
    dlogit = jnp.sum(places[:, :, None] * dshare.reshape(1, -1, tok_rows), axis=1)
    mixed.rider = dlogit.reshape(1, -1)
    pins = mixed.spread([gate_grad], weight)
    half = features // 2
    middle = half // 2
    tile = middle
    keep, send = rows_back(core, gate_grad, up_grad, w_gate, w_up, 0, middle, tile, pins)
    pins = mixed.cross([keep])
    left = Reduction(keep, after(send, pins), tok_rows, odd)
    keep, send = rows_back(core, gate_grad, up_grad, w_gate, w_up, middle, half, tile, pins)
    pins = mixed.halve([keep])
    left.spread_part(0, pins)
    right = Reduction(keep, after(send, left.keep), tok_rows, odd)
    pins = right.spread_part(1, [])
    grad_down = outer(hidden, all_grads, pins)
    pins = left.cross_part(0, [grad_down])
    pins = pins + mixed.step(2, [grad_down])
    pins = pins + right.cross_part(1, [grad_down])
    grad_gate = outer(all_tokens, gate_grad, pins)
    pins = left.halve_part([grad_gate])
    pins = pins + mixed.step(1, [grad_gate])
    pins = pins + right.halve_part([grad_gate])
    grad_up = outer(all_tokens, up_grad, pins)
    pins = left.step(2, [grad_up])
    pins = pins + mixed.join([grad_up])
    pins = pins + right.step(2, [grad_up])
    side = core.reshape(1, 1)
    mixed_out, dlogit = finish([mixed], side, (), pins, "finish_mixed")
    dlogit = dlogit.reshape(-1, tok_rows)

    dlogit = jnp.sum(places[:, :, None] * dlogit[:, None, :], axis=0)
    sign = jnp.swapaxes(small[:, 2 * experts :], 1, 2)
    grad_logits = (sign * dlogit[:, :, None]).reshape(-1, experts)
    pieces = jnp.concatenate(split3(grad_logits), axis=1)
    grad_router = jnp.einsum("rd,re->de", all_tokens, pieces, preferred_element_type=jnp.float32)
    grad_router = (
        grad_router[:, 2 * experts :] + grad_router[:, experts : 2 * experts]
    ) + grad_router[:, :experts]
    left.step(1, [grad_router])
    right.step(1, left.keep)
    left.join(right.keep)
    right.join([])
    extra = (grad_logits[:tok_rows], w_router.T)
    (grad_tokens,) = finish([left, right], side, extra, [], "finish_tokens")
    return mixed_out, grad_tokens, grad_router, grad_gate[None], grad_up[None], grad_down[None]


def in_pairs():
    return (
        lax.axis_size("dp") == 2 and lax.axis_size("expert") == 4 and lax.axis_size("mp") == 4
    )


def local(tokens, w_router, expert_ids, partner, gate_weight, up_weight, down_weight, grad_out):
    if in_pairs():
        return local_pairs(
            tokens, w_router, expert_ids, partner, gate_weight, up_weight, down_weight, grad_out
        )
    experts = w_router.shape[1]
    blocks = ("dp", "expert")
    all_tokens = lax.all_gather(tokens, blocks, axis=0, tiled=True)
    all_grads = lax.all_gather(grad_out, blocks, axis=0, tiled=True)
    weight, slope, sign = routing(tokens, w_router, expert_ids, partner)
    small = lax.all_gather(
        jnp.concatenate([weight, slope, sign], axis=1), blocks, axis=0, tiled=True
    )
    mine = (lax.iota(jnp.int32, experts) == lax.axis_index("expert")).astype(jnp.float32)
    weight_all = jnp.sum(small[:, :experts] * mine, axis=1, keepdims=True)
    slope_all = jnp.sum(small[:, experts : 2 * experts] * mine, axis=1)
    sign_all = small[:, 2 * experts :]

    w_gate = gate_weight[0]
    w_up = up_weight[0]
    w_down = down_weight[0]
    pre_gate = jnp.dot(all_tokens, w_gate, preferred_element_type=jnp.float32)
    pre_up = jnp.dot(all_tokens, w_up, preferred_element_type=jnp.float32)
    back = jnp.einsum("rd,fd->rf", all_grads, w_down, preferred_element_type=jnp.float32)
    sigmoid_gate = jax.nn.sigmoid(pre_gate)
    swished = pre_gate * sigmoid_gate
    hidden = swished * pre_up
    dshare = jnp.sum(hidden * back, axis=1)
    hidden = (weight_all * hidden).astype(jnp.bfloat16)
    dhidden = weight_all * back
    up_grad = (dhidden * swished).astype(jnp.bfloat16)
    gate_grad = (dhidden * pre_up * sigmoid_gate * (1.0 + pre_gate * (1.0 - sigmoid_gate))).astype(
        jnp.bfloat16
    )
    dlogit = lax.psum(slope_all * dshare, ("dp", "expert", "mp"))

    def collect(partial_value):
        own = lax.psum_scatter(
            partial_value.astype(jnp.bfloat16), blocks, scatter_dimension=0, tiled=True
        )
        return lax.psum(own, "mp")

    mixed = collect(jnp.dot(hidden, w_down, preferred_element_type=jnp.float32))
    row_grads = collect(
        jnp.einsum("rf,df->rd", gate_grad, w_gate, preferred_element_type=jnp.float32)
        + jnp.einsum("rf,df->rd", up_grad, w_up, preferred_element_type=jnp.float32)
    )
    grad_down = jnp.einsum("rf,rd->fd", hidden, all_grads, preferred_element_type=jnp.float32)
    grad_gate = jnp.einsum("rd,rf->df", all_tokens, gate_grad, preferred_element_type=jnp.float32)
    grad_up = jnp.einsum("rd,rf->df", all_tokens, up_grad, preferred_element_type=jnp.float32)

    grad_logits = sign_all * dlogit[:, None]
    pieces = jnp.concatenate(split3(grad_logits), axis=1)
    grad_router = jnp.einsum("rd,re->de", all_tokens, pieces, preferred_element_type=jnp.float32)
    grad_router = (
        grad_router[:, 2 * experts :] + grad_router[:, experts : 2 * experts]
    ) + grad_router[:, :experts]
    tok_rows = tokens.shape[0]
    block = lax.axis_index("dp") * lax.axis_size("expert") + lax.axis_index("expert")
    own_logits = lax.dynamic_slice_in_dim(grad_logits, block * tok_rows, tok_rows, 0)
    router_back = jnp.dot(own_logits, w_router.T, precision=lax.Precision.HIGHEST)
    grad_tokens = (router_back + row_grads.astype(jnp.float32)).astype(jnp.bfloat16)
    return (
        mixed,
        grad_tokens,
        grad_router,
        grad_gate.astype(jnp.bfloat16)[None],
        grad_up.astype(jnp.bfloat16)[None],
        grad_down.astype(jnp.bfloat16)[None],
    )


def solution(mesh):
    in_specs = (
        P(("dp", "expert"), None),
        P(),
        P(("dp", "expert"), None),
        P(),
        P("expert", None, ("dp", "mp")),
        P("expert", None, ("dp", "mp")),
        P("expert", ("dp", "mp"), None),
        P(("dp", "expert"), None),
    )
    out_specs = (
        P(("dp", "expert"), None),
        P(("dp", "expert"), None),
        P(),
        P("expert", None, ("dp", "mp")),
        P("expert", None, ("dp", "mp")),
        P("expert", ("dp", "mp"), None),
    )
    return jax.shard_map(local, mesh=mesh, in_specs=in_specs, out_specs=out_specs, check_vma=False)
```

```python
import functools

import jax
import jax.numpy as jnp
from jax import lax
from jax.experimental import pallas as pl
from jax.experimental.pallas import tpu as pltpu
from jax.sharding import PartitionSpec as P


def split3(values):
    high = values.astype(jnp.bfloat16)
    rest = values - high.astype(jnp.float32)
    middle = rest.astype(jnp.bfloat16)
    low = (rest - middle.astype(jnp.float32)).astype(jnp.bfloat16)
    return high, middle, low


def routing(tokens, w_router, expert_ids, partner):
    tok_rows = tokens.shape[0]
    experts = w_router.shape[1]
    slot_count = min(tok_rows, 4 * tok_rows // experts)
    keep_count = 3 * slot_count // 4
    pieces = jnp.concatenate(split3(w_router), axis=1)
    logits = jnp.dot(tokens, pieces, preferred_element_type=jnp.float32)
    logits = logits.reshape(tok_rows, 3, experts)
    logits = (logits[:, 2] + logits[:, 1]) + logits[:, 0]
    columns = lax.broadcasted_iota(jnp.int32, (tok_rows, experts), 1)
    first = expert_ids[:, :1] == columns
    second = expert_ids[:, 1:] == columns
    first_float = first.astype(jnp.float32)
    second_float = second.astype(jnp.float32)
    difference = jnp.sum(logits * (first_float - second_float), axis=1, keepdims=True)
    share_one = jax.nn.sigmoid(difference)
    share_two = 1.0 - share_one
    rows = lax.broadcasted_iota(jnp.int32, (tok_rows, tok_rows), 0)
    before = (lax.broadcasted_iota(jnp.int32, (tok_rows, tok_rows), 1) < rows).astype(jnp.bfloat16)
    named = (first_float + second_float).astype(jnp.bfloat16)
    earlier = jnp.dot(before, named, preferred_element_type=jnp.float32)
    arrival_one = jnp.sum(earlier * first_float, axis=1, keepdims=True)
    arrival_two = jnp.sum(earlier * second_float, axis=1, keepdims=True)
    mate = partner[None, :]
    mate_one = jnp.sum(jnp.where(first, mate, 0), axis=1, keepdims=True)
    mate_two = jnp.sum(jnp.where(second, mate, 0), axis=1, keepdims=True)
    target_one = jnp.where(arrival_one < keep_count, expert_ids[:, :1], mate_one)
    target_two = jnp.where(arrival_two < keep_count, expert_ids[:, 1:], mate_two)
    lands_one = (target_one == columns).astype(jnp.float32)
    lands_two = (target_two == columns).astype(jnp.float32)
    weight = share_one * lands_one + share_two * lands_two
    slope = share_one * share_two * (lands_one - lands_two)
    return weight, slope, first_float - second_float


def swap(values, axis, flip):
    size = lax.axis_size(axis)
    return lax.ppermute(values, axis, [(place, place ^ flip) for place in range(size)])


NT = (((1,), (1,)), ((), ()))
TN = (((0,), (0,)), ((), ()))
WHOLE = pl.BlockSpec(memory_space=pltpu.VMEM)
LEFT = pl.BlockSpec(memory_space=pl.ANY)


def settings():
    return pltpu.CompilerParams(vmem_limit_bytes=40 << 20)


def after(values, pins):
    if not pins:
        return values
    return lax.optimization_barrier((values, *pins))[0]


def on_hbm(*arrays):
    return tuple(pltpu.with_memory_space_constraint(array, pltpu.HBM) for array in arrays)


def in_hbm(shape, dtype=jnp.bfloat16):
    return pltpu.HBM(shape, dtype)


def in_vmem(shape, dtype=jnp.bfloat16):
    return pltpu.VMEM(shape, dtype)


def cost(flops, moved):
    return pl.CostEstimate(flops=flops, bytes_accessed=moved, transcendentals=0)


def once(shape):
    return pl.BlockSpec(shape, lambda i: (0,) * len(shape), pipeline_mode=pl.Buffered(1))


def shaped(shape, dtype=jnp.bfloat16):
    return jax.ShapeDtypeStruct(shape, dtype)


def routing_kernel(experts, keep_count, tokens, w_router, ids, partner, out):
    tok_rows = tokens.shape[0]
    high, middle, low = split3(w_router[...])

    def product(piece):
        return lax.dot_general(piece, tokens[...], NT, preferred_element_type=jnp.float32)

    logits = (product(low) + product(middle)) + product(high)
    names = lax.broadcasted_iota(jnp.int32, (experts, tok_rows), 0)
    first = (ids[0:1, :] == names).astype(jnp.float32)
    second = (ids[1:2, :] == names).astype(jnp.float32)
    difference = jnp.sum(logits * (first - second), axis=0, keepdims=True)
    share_one = jax.nn.sigmoid(difference)
    share_two = 1.0 - share_one
    source = lax.broadcasted_iota(jnp.int32, (tok_rows, tok_rows), 0)
    before = source < lax.broadcasted_iota(jnp.int32, (tok_rows, tok_rows), 1)
    earlier = jnp.dot(first + second, before.astype(jnp.float32), preferred_element_type=jnp.float32)
    arrival_one = jnp.sum(earlier * first, axis=0, keepdims=True)
    arrival_two = jnp.sum(earlier * second, axis=0, keepdims=True)
    mates = jnp.zeros(names.shape, jnp.int32)
    for expert in range(experts):
        mates = jnp.where(names == expert, partner[expert], mates)
    mates = mates.astype(jnp.float32)
    place = names.astype(jnp.float32)

    def lands(chosen, arrival):
        own = jnp.sum(chosen * place, axis=0, keepdims=True)
        mate = jnp.sum(chosen * mates, axis=0, keepdims=True)
        target = jnp.where(arrival < keep_count, own, mate)
        return (target == place).astype(jnp.float32)

    lands_one = lands(first, arrival_one)
    lands_two = lands(second, arrival_two)
    out[0:experts, :] = share_one * lands_one + share_two * lands_two
    out[experts : 2 * experts, :] = share_one * share_two * (lands_one - lands_two)
    out[2 * experts :, :] = first - second


def route(tokens, w_router, expert_ids, partner):
    tok_rows = tokens.shape[0]
    experts = w_router.shape[1]
    slot_count = min(tok_rows, 4 * tok_rows // experts)
    return pl.pallas_call(
        functools.partial(routing_kernel, experts, 3 * slot_count // 4),
        out_shape=shaped((3 * experts, tok_rows), jnp.float32),
        in_specs=[WHOLE] * 3 + [pl.BlockSpec(memory_space=pltpu.SMEM)],
        out_specs=WHOLE,
        name="route",
        cost_estimate=cost(1 << 20, 1 << 20),
    )(tokens, w_router.T, expert_ids.T, partner)


def tile_of(number, size):
    return pl.ds(pl.multiple_of(number * size, size), size)


class Mover:
    def __init__(self, sems):
        self.sems = sems
        self.used = 0

    def start(self, source, target):
        copy = pltpu.make_async_copy(source, target, self.sems.at[self.used])
        self.used += 1
        copy.start()
        return copy


def fetch_rows(mover, blocks, rows):
    count = blocks[0].shape[0]
    return [
        mover.start(block, rows.at[pl.ds(number * count, count), :])
        for number, block in enumerate(blocks)
    ]


def forward(blocks, w_gate, w_up, tile):
    number = len(blocks)
    tok_rows, features = blocks[0].shape
    count = number * tok_rows
    width = w_gate.shape[1]

    def body(*refs):
        pieces, refs = refs[:number], refs[number:]
        wg, wu, hid, sw, sg, everything, x, bg, bu, h, a, b, sems_in, sems_out = refs
        mover, outward = Mover(sems_in), Mover(sems_out)
        moves = fetch_rows(mover, pieces, x)
        tiles = [pl.ds(step * tile, tile) for step in range(width // tile)]
        copies = [
            (
                mover.start(wg.at[:, place], bg.at[:, place]),
                mover.start(wu.at[:, place], bu.at[:, place]),
            )
            for place in tiles
        ]
        for copy in moves:
            copy.wait()
        done = []
        for place, pair in zip(tiles, copies):
            for copy in pair:
                copy.wait()
            if pair is copies[-1]:
                done.append(outward.start(x, everything))
            gate = jnp.dot(x[...], bg[:, place], preferred_element_type=jnp.float32)
            up = jnp.dot(x[...], bu[:, place], preferred_element_type=jnp.float32)
            sigmoid_gate = jax.nn.sigmoid(gate)
            swished = gate * sigmoid_gate
            h[:, place] = (swished * up).astype(jnp.bfloat16)
            a[:, place] = swished.astype(jnp.bfloat16)
            b[:, place] = (up * sigmoid_gate * (1.0 + gate * (1.0 - sigmoid_gate))).astype(
                jnp.bfloat16
            )
        done += [outward.start(h, hid), outward.start(a, sw), outward.start(b, sg)]
        for copy in done:
            copy.wait()

    flat = pltpu.VMEM((count, width), jnp.bfloat16)
    weights = pltpu.VMEM((features, width), jnp.bfloat16)
    return pl.pallas_call(
        body,
        out_shape=(in_hbm((count, width)),) * 3 + (in_hbm((count, features)),),
        in_specs=[LEFT] * (number + 2),
        out_specs=(LEFT,) * 4,
        scratch_shapes=[
            pltpu.VMEM((count, features), jnp.bfloat16),
            weights,
            weights,
            flat,
            flat,
            flat,
            pltpu.SemaphoreType.DMA((number + 2 * (width // tile),)),
            pltpu.SemaphoreType.DMA((4,)),
        ],
        compiler_params=pltpu.CompilerParams(vmem_limit_bytes=40 << 20),
        name="forward",
        cost_estimate=cost(4 * count * features * width, 6 * features * width),
    )(*on_hbm(*blocks, w_gate, w_up))


def down(core, hidden, w_down, tile, pins):
    count, width = hidden.shape
    half = w_down.shape[1] // 2
    steps = half // tile
    hidden = after(hidden, pins)

    def body(core_ref, hid, wd, keep, send, h, bd, k, s, sems_in, sems_out):
        mover, outward = Mover(sems_in), Mover(sems_out)
        copies = [mover.start(hid, h), mover.start(wd, bd)]
        for copy in copies:
            copy.wait()
        me = core_ref[0]
        done = []
        for side, target, out in ((1 - me, s, send), (me, k, keep)):
            for step in range(steps):
                source = pl.ds(pl.multiple_of(side * half + step * tile, tile), tile)
                columns = pl.ds(step * tile, tile)
                target[:, columns] = jnp.dot(
                    h[...], bd[:, source], preferred_element_type=jnp.float32
                ).astype(jnp.bfloat16)
                done.append(outward.start(target.at[:, columns], out.at[:, columns]))
        for copy in done:
            copy.wait()

    part = pltpu.VMEM((count, half), jnp.bfloat16)
    return pl.pallas_call(
        body,
        out_shape=(in_hbm((count, half)),) * 2,
        in_specs=[pl.BlockSpec(memory_space=pltpu.SMEM)] + [LEFT] * 2,
        out_specs=(LEFT,) * 2,
        scratch_shapes=[
            pltpu.VMEM((count, width), jnp.bfloat16),
            pltpu.VMEM((width, 2 * half), jnp.bfloat16),
            part,
            part,
            pltpu.SemaphoreType.DMA((2,)),
            pltpu.SemaphoreType.DMA((2 * steps,)),
        ],
        compiler_params=pltpu.CompilerParams(vmem_limit_bytes=24 << 20),
        name="down",
        cost_estimate=cost(4 * count * half * width, 4 * half * width),
    )(core, *on_hbm(hidden, w_down))


def backward(blocks, w_down, hidden, sw, sg, weight, slope, tile):
    number = len(blocks)
    tok_rows, features = blocks[0].shape
    count = number * tok_rows
    width = w_down.shape[0]

    def body(*refs):
        pieces, refs = refs[:number], refs[number:]
        wd, hid, swished, slopes, c, v, up_out, gate_out, hidden_out, ds, everything = refs[:11]
        x, bd, h, a, b, ug, gg, hc, sems_in, sems_out = refs[11:]
        mover, outward = Mover(sems_in), Mover(sems_out)
        moves = fetch_rows(mover, pieces, x)
        tiles = [pl.ds(step * tile, tile) for step in range(width // tile)]
        copies = [mover.start(wd.at[tiles[0], :], bd.at[tiles[0], :])]
        for copy in moves:
            copy.wait()
        rest = [mover.start(hid, h), mover.start(swished, a), mover.start(slopes, b)]
        ds[...] = jnp.zeros_like(ds)
        scale = c[...]
        for step, place in enumerate(tiles):
            if step + 1 < len(tiles):
                following = tiles[step + 1]
                copies.append(mover.start(wd.at[following, :], bd.at[following, :]))
            copies[step].wait()
            if step == 0:
                done = [outward.start(x, everything)]
            back = lax.dot_general(x[...], bd[place, :], NT, preferred_element_type=jnp.float32)
            if step == 0:
                for copy in rest:
                    copy.wait()
            value = h[:, place].astype(jnp.float32)
            ds[...] += jnp.sum(value * back, axis=1, keepdims=True) * v[...]
            hc[:, place] = (value * scale).astype(jnp.bfloat16)
            back = back * scale
            ug[:, place] = (back * a[:, place].astype(jnp.float32)).astype(jnp.bfloat16)
            gg[:, place] = (back * b[:, place].astype(jnp.float32)).astype(jnp.bfloat16)
        done += [
            outward.start(ug, up_out),
            outward.start(gg, gate_out),
            outward.start(hc, hidden_out),
        ]
        for copy in done:
            copy.wait()

    flat = pltpu.VMEM((count, width), jnp.bfloat16)
    return pl.pallas_call(
        body,
        out_shape=(in_hbm((count, width)),) * 3
        + (shaped((count, 1), jnp.float32), in_hbm((count, features))),
        in_specs=[LEFT] * (number + 4) + [WHOLE] * 2,
        out_specs=(LEFT,) * 3 + (WHOLE, LEFT),
        scratch_shapes=[
            pltpu.VMEM((count, features), jnp.bfloat16),
            pltpu.VMEM((width, features), jnp.bfloat16),
        ]
        + [flat] * 6
        + [
            pltpu.SemaphoreType.DMA((number + width // tile + 3,)),
            pltpu.SemaphoreType.DMA((4,)),
        ],
        compiler_params=pltpu.CompilerParams(vmem_limit_bytes=40 << 20),
        name="backward",
        cost_estimate=cost(2 * count * features * width, 2 * features * width),
    )(*on_hbm(*blocks, w_down, hidden, sw, sg), weight, slope)


def rows_back(core, gate_grad, up_grad, w_gate, w_up, first, last, tile, pins, rider=None):
    count, width = gate_grad.shape
    half = w_gate.shape[0] // 2
    gate_grad = after(gate_grad, pins)
    steps = (last - first) // tile

    riders = [] if rider is None else [rider]
    tail = TAIL * len(riders)

    def body(core_ref, gate_in, up_in, wg, wu, *refs):
        keep, send, gg, ug, bg, bu, k, s, sems_in, sems_out = refs[len(riders) :]
        if riders:
            s[count:, : rider.shape[1]] = pack(refs[0][...])
        mover, outward = Mover(sems_in), Mover(sems_out)
        me = core_ref[0]
        pieces = []
        for side, target, out in ((1 - me, s, send), (me, k, keep)):
            for step in range(steps):
                source = pl.ds(pl.multiple_of(side * half + first + step * tile, tile), tile)
                pieces.append((source, target, pl.ds(step * tile, tile), out))
        copies = []

        def load(number):
            if number < len(pieces):
                source, place = pieces[number][0], pl.ds(number * tile, tile)
                copies.append(mover.start(wg.at[source, :], bg.at[place, :]))
                copies.append(mover.start(wu.at[source, :], bu.at[place, :]))

        rows = [mover.start(gate_in, gg), mover.start(up_in, ug)]
        load(0)
        for copy in rows:
            copy.wait()
        done = []
        for number, (_, target, columns, out) in enumerate(pieces):
            load(number + 1)
            place = pl.ds(number * tile, tile)
            copies[2 * number].wait()
            total = lax.dot_general(gg[...], bg[place, :], NT, preferred_element_type=jnp.float32)
            copies[2 * number + 1].wait()
            total = total + lax.dot_general(
                ug[...], bu[place, :], NT, preferred_element_type=jnp.float32
            )
            target[:count, columns] = total.astype(jnp.bfloat16)
            done.append(outward.start(target.at[:, columns], out.at[:, columns]))
        for copy in done:
            copy.wait()

    flat = pltpu.VMEM((count, width), jnp.bfloat16)
    weights = pltpu.VMEM((2 * (last - first), width), jnp.bfloat16)
    part = pltpu.VMEM((count, last - first), jnp.bfloat16)
    sent = (count + tail, last - first)
    return pl.pallas_call(
        body,
        out_shape=(in_hbm((count, last - first)), in_hbm(sent)),
        in_specs=[pl.BlockSpec(memory_space=pltpu.SMEM)] + [LEFT] * 4 + [WHOLE] * len(riders),
        out_specs=(LEFT,) * 2,
        scratch_shapes=[flat, flat, weights, weights, part, pltpu.VMEM(sent, jnp.bfloat16)]
        + [pltpu.SemaphoreType.DMA((4 * steps + 2,)), pltpu.SemaphoreType.DMA((2 * steps,))],
        compiler_params=pltpu.CompilerParams(vmem_limit_bytes=40 << 20),
        name="rows_back",
        cost_estimate=cost(8 * count * (last - first) * width, 8 * (last - first) * width),
    )(core, *on_hbm(gate_grad, up_grad, w_gate, w_up), *riders)


def outer(left, right, pins):
    left = after(left, pins)
    return lax.dot_general(left, right, TN, preferred_element_type=jnp.float32).astype(jnp.bfloat16)


def small_call(body, outs, args, pins, name):
    first = after(args[0], pins)
    return pl.pallas_call(
        body,
        out_shape=tuple(outs),
        in_specs=[WHOLE] * len(args),
        out_specs=(WHOLE,) * len(outs),
        compiler_params=settings(),
        name=name,
        cost_estimate=cost(1 << 20, 1 << 20),
    )(first, *args[1:])


def add(one, two):
    return (one.astype(jnp.float32) + two.astype(jnp.float32)).astype(jnp.bfloat16)


def trade(values, kind):
    cores, experts = lax.axis_size("dp"), lax.axis_size("expert")
    pairs = []
    for core in range(cores):
        for place in range(experts):
            flip = {"peer": 0, "first": 1 + core, "second": 2 - core, "both": 3}[kind]
            other = core ^ 1 if kind == "peer" else core
            pairs.append((core * experts + place, other * experts + (place ^ flip)))
    return lax.ppermute(values, ("dp", "expert"), pairs)


TAIL = 16


def pack(values):
    count, length = values.shape
    row = lax.broadcasted_iota(jnp.int32, (TAIL, length), 0)
    out = jnp.zeros((TAIL, length), jnp.float32)
    for number, piece in enumerate(split3(values)):
        for place in range(count):
            line = piece[place : place + 1, :].astype(jnp.float32)
            out = jnp.where(row == number * count + place, line, out)
    return out.astype(jnp.bfloat16)


def unpack(block, count):
    block = block.astype(jnp.float32)
    row = lax.broadcasted_iota(jnp.int32, block.shape, 0)
    line = lax.broadcasted_iota(jnp.int32, (count, block.shape[1]), 0)
    out = jnp.zeros((count, block.shape[1]), jnp.float32)
    for place in range(count):
        picked = (row == place) | (row == count + place) | (row == 2 * count + place)
        total = jnp.sum(jnp.where(picked, block, 0.0), axis=0, keepdims=True)
        out = jnp.where(line == place, total, out)
    return out


class Reduction:
    def __init__(self, keep, send, tok_rows, odd, rider=None):
        self.rows = tok_rows
        self.width = keep.shape[1]
        self.keep = (keep,)
        self.odd = odd
        self.rider = rider
        self.arrived = (trade(send, "peer"),)

    def spread_part(self, number, pins):
        rows = self.rows

        def body(inputs, sent, kept):
            keep, arrived = inputs
            for side in range(2):
                for place, there in enumerate((0, 2, 1, 3)):
                    away = place in ((1, 3), (2, 3))[number]
                    slot = 2 * side + (place // 2, place % 2)[number]
                    (sent if away else kept)[0][pl.ds(slot * rows, rows), :] = add(
                        keep[pl.ds((4 * side + place) * rows, rows), :],
                        arrived[pl.ds((4 * (1 - side) + there) * rows, rows), :],
                    )

        shape = (4 * rows, self.width)
        sent = self.run(body, [shape], [shape], [], pins, "spread_part", True)
        self.arrived = (trade(sent[0], ("first", "second")[number]),)
        return list(self.keep)

    def cross_part(self, number, pins):
        rows = self.rows

        def body(inputs, sent, kept):
            keep, arrived = inputs
            for place in range(4):
                out = (sent if place % 2 else kept)[0]
                source = pl.ds(place * rows, rows)
                out[pl.ds(place // 2 * rows, rows), :] = add(keep[source, :], arrived[source, :])

        shape = (2 * rows, self.width)
        sent = self.run(body, [shape], [shape], [], pins, "cross_part", True)
        self.arrived = (trade(sent[0], ("second", "first")[number]),)
        return list(self.keep)

    def halve_part(self, pins):
        rows, half = 2 * self.rows, self.width // 2

        def body(inputs, sent, kept):
            one = add(inputs[0][:, :half], inputs[1][:rows, :half])
            two = add(inputs[0][:, half:], inputs[1][:rows, half:])
            flag = inputs[2][...] > 0
            sent[0][:rows, :] = jnp.where(flag, one, two)
            kept[0][...] = jnp.where(flag, two, one)

        shape = (rows, half)
        sent = self.run(body, [shape], [shape], [self.odd], pins, "halve_part", True)
        self.arrived = (swap(sent[0], "mp", 1),)
        return list(self.keep)

    def run(self, body, sent, kept, extra, pins, name, rides):
        riding = self.rider is not None
        outs = [
            shaped((rows + (TAIL if riding and number == 0 else 0), width))
            for number, (rows, width) in enumerate(sent)
        ]
        outs += [shaped(shape) for shape in kept]
        args = [*self.keep, *self.arrived, *extra]
        tail_at = len(self.keep)
        if riding:
            args.append(self.rider)
            outs.append(shaped(self.rider.shape, jnp.float32))

        def whole(*refs):
            inputs, outputs = refs[: len(args)], refs[len(args) :]
            given = inputs[:-1] if riding else inputs
            body(given, outputs[: len(sent)], outputs[len(sent) : len(sent) + len(kept)])
            if riding:
                total = inputs[-1][...]
                length = total.shape[1]
                if rides:
                    arrived = inputs[tail_at]
                    block = arrived[arrived.shape[0] - TAIL :, :length]
                    total = total + unpack(block, total.shape[0])
                outputs[-1][...] = total
                outputs[0][sent[0][0] :, :length] = pack(total)

        outs = small_call(whole, outs, args, pins, name)
        if riding:
            self.rider = outs[-1]
        self.keep = outs[len(sent) : len(sent) + len(kept)] if kept else (outs[0],)
        return outs[: len(sent)]

    def spread(self, pins, scale=None):
        rows, half = self.rows, self.width // 2

        def body(inputs, sent, kept):
            keep, arrived = inputs[0], inputs[1]
            for side in range(2):
                for place, there in enumerate((0, 2, 1, 3)):
                    source = pl.ds((4 * side + place) * rows, rows)
                    total = keep[source, :].astype(jnp.float32) + arrived[
                        pl.ds((4 * (1 - side) + there) * rows, rows), :
                    ].astype(jnp.float32)
                    if scale is not None:
                        total = total * inputs[2][source, :]
                    total = total.astype(jnp.bfloat16)
                    left = pl.ds((2 * side + place // 2) * rows, rows)
                    right = pl.ds((2 * side + place % 2) * rows, rows)
                    (sent if place in (1, 3) else kept)[0][left, :] = total[:, :half]
                    (sent if place in (2, 3) else kept)[1][right, :] = total[:, half:]

        extra = [] if scale is None else [scale]
        shape = (4 * rows, half)
        sent = self.run(body, [shape] * 2, [shape] * 2, extra, pins, "spread", False)
        self.arrived = (trade(sent[0], "first"), trade(sent[1], "second"))
        return list(self.keep[:1])

    def cross(self, pins):
        rows, half = self.rows, self.width // 2

        def body(inputs, sent, kept):
            for part in range(2):
                keep, arrived = inputs[part], inputs[2 + part]
                for place in range(4):
                    out = (sent if place % 2 else kept)[part]
                    source = pl.ds(place * rows, rows)
                    out[pl.ds(place // 2 * rows, rows), :] = add(
                        keep[source, :], arrived[source, :]
                    )

        shape = (2 * rows, half)
        sent = self.run(body, [shape] * 2, [shape] * 2, [], pins, "cross", True)
        self.arrived = (trade(sent[0], "second"), trade(sent[1], "first"))
        return list(self.keep[:1])

    def halve(self, pins):
        rows, half = 2 * self.rows, self.width // 2

        def body(inputs, sent, kept):
            one = add(inputs[0][...], inputs[2][:rows, :])
            two = add(inputs[1][...], inputs[3][...])
            flag = inputs[4][...] > 0
            sent[0][:rows, :] = jnp.where(flag, one, two)
            kept[0][...] = jnp.where(flag, two, one)

        shape = (rows, half)
        sent = self.run(body, [shape], [shape], [self.odd], pins, "halve", True)
        self.arrived = (swap(sent[0], "mp", 1),)
        return list(self.keep)

    def step(self, flip, pins):
        rows, half = 2 * self.rows, self.width // 2

        def body(inputs, sent, kept):
            sent[0][:rows, :] = add(inputs[0][:rows, :], inputs[1][:rows, :])

        sent = self.run(body, [(rows, half)], [], [], pins, "step", True)
        self.arrived = (swap(sent[0], "mp", flip),)
        return list(self.keep)

    def join(self, pins):
        rows, half = self.rows, self.width // 2

        def body(inputs, sent, kept):
            keep, arrived = inputs[0], inputs[1]
            flag = inputs[2][...] > 0
            for out, place in ((kept[0], pl.ds(0, rows)), (sent[0], pl.ds(rows, rows))):
                out[:rows, :half] = jnp.where(flag, arrived[place, :], keep[place, :])
                out[:rows, half:] = jnp.where(flag, keep[place, :], arrived[place, :])

        shape = (rows, self.width)
        sent = self.run(body, [shape], [shape], [self.odd], pins, "join", False)
        self.arrived = (trade(sent[0], "peer"),)
        return list(self.keep)


def meet(sums, pins):
    sizes = [len(item.arrived) for item in sums]
    held = lax.optimization_barrier(
        (*[array for item in sums for array in item.arrived], *pins)
    )
    for item, size in zip(sums, sizes):
        item.arrived, held = held[:size], held[size:]


def finish(parts, core, extra, pins, name):
    rows, width = parts[0].keep[0].shape
    features = 2 * width * len(parts)
    args = [item for part in parts for item in (part.keep[0], part.arrived[0])]
    at = len(args)
    args += [core, *extra]

    def body(*refs):
        out = refs[len(args)]
        flag = refs[at][...] > 0
        for number in range(len(parts)):
            keep, arrived = refs[2 * number][...], refs[2 * number + 1][:rows, :]
            sides = (jnp.where(flag, arrived, keep), jnp.where(flag, keep, arrived))
            for side, values in enumerate(sides):
                columns = pl.ds(side * features // 2 + number * width, width)
                if extra:
                    values = values.astype(jnp.float32)
                    logits, router = refs[at + 1], refs[at + 2]
                    for expert in range(router.shape[0]):
                        values = values + logits[:, expert : expert + 1] * (
                            router[expert : expert + 1, columns]
                        )
                out[:, columns] = values.astype(jnp.bfloat16)

    return small_call(body, [shaped((rows, features))], args, pins, name)[0]


def gather_rows(block, peer, near, second, far):
    near_peer, second_peer = trade(second, "peer"), trade(near, "peer")
    return [block, near, second, far, peer, near_peer, second_peer, trade(far, "peer")]


def swapped(blocks):
    return jnp.stack([blocks[0], blocks[2], blocks[1], blocks[3]])


def gather_small(small):
    found = jnp.stack([small, trade(small, "first")])
    return jnp.concatenate([found, trade(found, "second")], axis=0)


def order():
    core, expert = lax.axis_index("dp"), lax.axis_index("expert")
    flips = (0, 1 + core, 2 - core, 3)
    places = [(core ^ side) * 4 + (expert ^ flip) for side in range(2) for flip in flips]
    places = jnp.stack([jnp.asarray(place, jnp.int32) for place in places])
    return (lax.iota(jnp.int32, 8)[:, None] == places[None, :]).astype(jnp.float32)


def local_pairs(tokens, w_router, expert_ids, partner, gate_weight, up_weight, down_weight, grad_out):
    tok_rows, features = tokens.shape
    experts = w_router.shape[1]
    width = gate_weight.shape[2]
    w_gate, w_up, w_down = gate_weight[0], up_weight[0], down_weight[0]
    odd = (lax.axis_index("mp") & 1).astype(jnp.int32).reshape(1, 1)
    core = lax.axis_index("dp").astype(jnp.int32).reshape(1)

    tok_near = trade(tokens, "first")
    tok_second = trade(tokens, "second")
    tok_peer = trade(tokens, "peer")
    small = route(tokens, w_router, expert_ids, partner)
    tok_far = trade(after(tok_near, [small]), "second")
    small = gather_small(small)
    small_peer = trade(small, "peer")
    token_blocks = gather_rows(tokens, tok_peer, tok_near, tok_second, after(tok_far, [small]))
    later = after(grad_out, [tok_far])
    out_near = trade(later, "first")
    out_second = trade(later, "second")
    out_far = trade(later, "both")
    out_peer = trade(grad_out, "peer")
    small = jnp.concatenate([small, swapped(small_peer)], axis=0)
    mine = (lax.iota(jnp.int32, experts) == lax.axis_index("expert")).astype(jnp.float32)
    mine = mine[None, :, None]
    weight = jnp.sum(small[:, :experts] * mine, axis=1).reshape(-1, 1)
    slope = jnp.sum(small[:, experts : 2 * experts] * mine, axis=1).reshape(-1, 1)
    token_blocks[0] = after(token_blocks[0], [weight, slope])
    hidden, sw, sg, all_tokens = forward(token_blocks, w_gate, w_up, width // 4)
    keep, send = down(core, hidden, w_down, features // 4, [])
    out_near, out_second, out_far = (
        after(item, [keep]) for item in (out_near, out_second, out_far)
    )
    grad_blocks = gather_rows(grad_out, out_peer, out_near, out_second, out_far)
    send = after(send, [out_near, out_second, out_far])
    mixed = Reduction(keep, send, tok_rows, odd)
    grad_blocks[0] = after(grad_blocks[0], mixed.spread([], weight))
    up_grad, gate_grad, hidden, dshare, all_grads = backward(
        grad_blocks, w_down, hidden, sw, sg, weight, slope, width // 2
    )
    places = order()
    dlogit = jnp.sum(places[:, :, None] * dshare.reshape(1, -1, tok_rows), axis=1)
    dlogit = dlogit.reshape(2, -1)
    meet([mixed], [gate_grad])
    pins = mixed.cross([])
    half = features // 2
    middle = half // 2
    tile = middle
    keep, send = rows_back(
        core, gate_grad, up_grad, w_gate, w_up, 0, middle, tile, pins, dlogit
    )
    meet([mixed], [keep])
    pins = mixed.halve([])
    left = Reduction(keep, after(send, pins), tok_rows, odd, dlogit)
    keep, send = rows_back(core, gate_grad, up_grad, w_gate, w_up, middle, half, tile, pins)
    meet([mixed, left], [keep])
    pins = left.spread_part(0, [])
    right = Reduction(keep, after(send, pins), tok_rows, odd)
    pins = mixed.step(2, pins)
    pins = pins + right.spread_part(1, [])
    grad_down = outer(hidden, all_grads, pins)
    meet([left, right, mixed], [grad_down])
    pins = left.cross_part(0, []) + right.cross_part(1, [])
    pins = mixed.step(1, pins)
    grad_gate = outer(all_tokens, gate_grad, pins)
    meet([left, right, mixed], [grad_gate])
    pins = left.halve_part([]) + right.halve_part([])
    pins = mixed.join(pins)
    grad_up = outer(all_tokens, up_grad, pins)
    meet([left, right], [grad_up])
    pins = left.step(2, []) + right.step(2, [])
    side = core.reshape(1, 1)
    mixed_out = finish([mixed], side, (), pins, "finish_mixed")
    meet([left, right], [mixed_out])
    left.step(1, [])
    right.step(1, [])
    dlogit = left.rider.reshape(-1, tok_rows)
    left.rider = None
    dlogit = jnp.sum(places[:, :, None] * dlogit[:, None, :], axis=0)
    sign = jnp.swapaxes(small[:, 2 * experts :], 1, 2)
    grad_logits = (sign * dlogit[:, :, None]).reshape(-1, experts)
    pieces = jnp.concatenate(split3(grad_logits), axis=1)
    grad_router = jnp.einsum("rd,re->de", all_tokens, pieces, preferred_element_type=jnp.float32)
    grad_router = (
        grad_router[:, 2 * experts :] + grad_router[:, experts : 2 * experts]
    ) + grad_router[:, :experts]
    meet([left, right], [grad_router])
    left.join([])
    right.join([])
    extra = (grad_logits[:tok_rows], w_router.T)
    grad_tokens = finish([left, right], side, extra, [], "finish_tokens")
    return mixed_out, grad_tokens, grad_router, grad_gate[None], grad_up[None], grad_down[None]


def in_pairs():
    return (
        lax.axis_size("dp") == 2 and lax.axis_size("expert") == 4 and lax.axis_size("mp") == 4
    )


def local(tokens, w_router, expert_ids, partner, gate_weight, up_weight, down_weight, grad_out):
    if in_pairs():
        return local_pairs(
            tokens, w_router, expert_ids, partner, gate_weight, up_weight, down_weight, grad_out
        )
    experts = w_router.shape[1]
    blocks = ("dp", "expert")
    all_tokens = lax.all_gather(tokens, blocks, axis=0, tiled=True)
    all_grads = lax.all_gather(grad_out, blocks, axis=0, tiled=True)
    weight, slope, sign = routing(tokens, w_router, expert_ids, partner)
    small = lax.all_gather(
        jnp.concatenate([weight, slope, sign], axis=1), blocks, axis=0, tiled=True
    )
    mine = (lax.iota(jnp.int32, experts) == lax.axis_index("expert")).astype(jnp.float32)
    weight_all = jnp.sum(small[:, :experts] * mine, axis=1, keepdims=True)
    slope_all = jnp.sum(small[:, experts : 2 * experts] * mine, axis=1)
    sign_all = small[:, 2 * experts :]

    w_gate = gate_weight[0]
    w_up = up_weight[0]
    w_down = down_weight[0]
    pre_gate = jnp.dot(all_tokens, w_gate, preferred_element_type=jnp.float32)
    pre_up = jnp.dot(all_tokens, w_up, preferred_element_type=jnp.float32)
    back = jnp.einsum("rd,fd->rf", all_grads, w_down, preferred_element_type=jnp.float32)
    sigmoid_gate = jax.nn.sigmoid(pre_gate)
    swished = pre_gate * sigmoid_gate
    hidden = swished * pre_up
    dshare = jnp.sum(hidden * back, axis=1)
    hidden = (weight_all * hidden).astype(jnp.bfloat16)
    dhidden = weight_all * back
    up_grad = (dhidden * swished).astype(jnp.bfloat16)
    gate_grad = (dhidden * pre_up * sigmoid_gate * (1.0 + pre_gate * (1.0 - sigmoid_gate))).astype(
        jnp.bfloat16
    )
    dlogit = lax.psum(slope_all * dshare, ("dp", "expert", "mp"))

    def collect(partial_value):
        own = lax.psum_scatter(
            partial_value.astype(jnp.bfloat16), blocks, scatter_dimension=0, tiled=True
        )
        return lax.psum(own, "mp")

    mixed = collect(jnp.dot(hidden, w_down, preferred_element_type=jnp.float32))
    row_grads = collect(
        jnp.einsum("rf,df->rd", gate_grad, w_gate, preferred_element_type=jnp.float32)
        + jnp.einsum("rf,df->rd", up_grad, w_up, preferred_element_type=jnp.float32)
    )
    grad_down = jnp.einsum("rf,rd->fd", hidden, all_grads, preferred_element_type=jnp.float32)
    grad_gate = jnp.einsum("rd,rf->df", all_tokens, gate_grad, preferred_element_type=jnp.float32)
    grad_up = jnp.einsum("rd,rf->df", all_tokens, up_grad, preferred_element_type=jnp.float32)

    grad_logits = sign_all * dlogit[:, None]
    pieces = jnp.concatenate(split3(grad_logits), axis=1)
    grad_router = jnp.einsum("rd,re->de", all_tokens, pieces, preferred_element_type=jnp.float32)
    grad_router = (
        grad_router[:, 2 * experts :] + grad_router[:, experts : 2 * experts]
    ) + grad_router[:, :experts]
    tok_rows = tokens.shape[0]
    block = lax.axis_index("dp") * lax.axis_size("expert") + lax.axis_index("expert")
    own_logits = lax.dynamic_slice_in_dim(grad_logits, block * tok_rows, tok_rows, 0)
    router_back = jnp.dot(own_logits, w_router.T, precision=lax.Precision.HIGHEST)
    grad_tokens = (router_back + row_grads.astype(jnp.float32)).astype(jnp.bfloat16)
    return (
        mixed,
        grad_tokens,
        grad_router,
        grad_gate.astype(jnp.bfloat16)[None],
        grad_up.astype(jnp.bfloat16)[None],
        grad_down.astype(jnp.bfloat16)[None],
    )


def solution(mesh):
    in_specs = (
        P(("dp", "expert"), None),
        P(),
        P(("dp", "expert"), None),
        P(),
        P("expert", None, ("dp", "mp")),
        P("expert", None, ("dp", "mp")),
        P("expert", ("dp", "mp"), None),
        P(("dp", "expert"), None),
    )
    out_specs = (
        P(("dp", "expert"), None),
        P(("dp", "expert"), None),
        P(),
        P("expert", None, ("dp", "mp")),
        P("expert", None, ("dp", "mp")),
        P("expert", ("dp", "mp"), None),
    )
    return jax.shard_map(local, mesh=mesh, in_specs=in_specs, out_specs=out_specs, check_vma=False)
```

```python
import functools

import jax
import jax.numpy as jnp
from jax import lax
from jax.experimental import pallas as pl
from jax.experimental.pallas import tpu as pltpu
from jax.sharding import PartitionSpec as P


def split3(values):
    high = values.astype(jnp.bfloat16)
    rest = values - high.astype(jnp.float32)
    middle = rest.astype(jnp.bfloat16)
    low = (rest - middle.astype(jnp.float32)).astype(jnp.bfloat16)
    return high, middle, low


def routing(tokens, w_router, expert_ids, partner):
    tok_rows = tokens.shape[0]
    experts = w_router.shape[1]
    slot_count = min(tok_rows, 4 * tok_rows // experts)
    keep_count = 3 * slot_count // 4
    pieces = jnp.concatenate(split3(w_router), axis=1)
    logits = jnp.dot(tokens, pieces, preferred_element_type=jnp.float32)
    logits = logits.reshape(tok_rows, 3, experts)
    logits = (logits[:, 2] + logits[:, 1]) + logits[:, 0]
    columns = lax.broadcasted_iota(jnp.int32, (tok_rows, experts), 1)
    first = expert_ids[:, :1] == columns
    second = expert_ids[:, 1:] == columns
    first_float = first.astype(jnp.float32)
    second_float = second.astype(jnp.float32)
    difference = jnp.sum(logits * (first_float - second_float), axis=1, keepdims=True)
    share_one = jax.nn.sigmoid(difference)
    share_two = 1.0 - share_one
    rows = lax.broadcasted_iota(jnp.int32, (tok_rows, tok_rows), 0)
    before = (lax.broadcasted_iota(jnp.int32, (tok_rows, tok_rows), 1) < rows).astype(jnp.bfloat16)
    named = (first_float + second_float).astype(jnp.bfloat16)
    earlier = jnp.dot(before, named, preferred_element_type=jnp.float32)
    arrival_one = jnp.sum(earlier * first_float, axis=1, keepdims=True)
    arrival_two = jnp.sum(earlier * second_float, axis=1, keepdims=True)
    mate = partner[None, :]
    mate_one = jnp.sum(jnp.where(first, mate, 0), axis=1, keepdims=True)
    mate_two = jnp.sum(jnp.where(second, mate, 0), axis=1, keepdims=True)
    target_one = jnp.where(arrival_one < keep_count, expert_ids[:, :1], mate_one)
    target_two = jnp.where(arrival_two < keep_count, expert_ids[:, 1:], mate_two)
    lands_one = (target_one == columns).astype(jnp.float32)
    lands_two = (target_two == columns).astype(jnp.float32)
    weight = share_one * lands_one + share_two * lands_two
    slope = share_one * share_two * (lands_one - lands_two)
    return weight, slope, first_float - second_float


def swap(values, axis, flip):
    size = lax.axis_size(axis)
    return lax.ppermute(values, axis, [(place, place ^ flip) for place in range(size)])


NT = (((1,), (1,)), ((), ()))
TN = (((0,), (0,)), ((), ()))
WHOLE = pl.BlockSpec(memory_space=pltpu.VMEM)
LEFT = pl.BlockSpec(memory_space=pl.ANY)


def settings():
    return pltpu.CompilerParams(vmem_limit_bytes=40 << 20)


def after(values, pins):
    if not pins:
        return values
    return lax.optimization_barrier((values, *pins))[0]


def on_hbm(*arrays):
    return tuple(pltpu.with_memory_space_constraint(array, pltpu.HBM) for array in arrays)


def in_hbm(shape, dtype=jnp.bfloat16):
    return pltpu.HBM(shape, dtype)


def in_vmem(shape, dtype=jnp.bfloat16):
    return pltpu.VMEM(shape, dtype)


def cost(flops, moved):
    return pl.CostEstimate(flops=flops, bytes_accessed=moved, transcendentals=0)


def once(shape):
    return pl.BlockSpec(shape, lambda i: (0,) * len(shape), pipeline_mode=pl.Buffered(1))


def shaped(shape, dtype=jnp.bfloat16):
    return jax.ShapeDtypeStruct(shape, dtype)


def routing_kernel(experts, keep_count, tokens, w_router, ids, partner, out):
    tok_rows = tokens.shape[0]
    high, middle, low = split3(w_router[...])

    def product(piece):
        return lax.dot_general(piece, tokens[...], NT, preferred_element_type=jnp.float32)

    logits = (product(low) + product(middle)) + product(high)
    names = lax.broadcasted_iota(jnp.int32, (experts, tok_rows), 0)
    first = (ids[0:1, :] == names).astype(jnp.float32)
    second = (ids[1:2, :] == names).astype(jnp.float32)
    difference = jnp.sum(logits * (first - second), axis=0, keepdims=True)
    share_one = jax.nn.sigmoid(difference)
    share_two = 1.0 - share_one
    source = lax.broadcasted_iota(jnp.int32, (tok_rows, tok_rows), 0)
    before = source < lax.broadcasted_iota(jnp.int32, (tok_rows, tok_rows), 1)
    earlier = jnp.dot(first + second, before.astype(jnp.float32), preferred_element_type=jnp.float32)
    arrival_one = jnp.sum(earlier * first, axis=0, keepdims=True)
    arrival_two = jnp.sum(earlier * second, axis=0, keepdims=True)
    mates = jnp.zeros(names.shape, jnp.int32)
    for expert in range(experts):
        mates = jnp.where(names == expert, partner[expert], mates)
    mates = mates.astype(jnp.float32)
    place = names.astype(jnp.float32)

    def lands(chosen, arrival):
        own = jnp.sum(chosen * place, axis=0, keepdims=True)
        mate = jnp.sum(chosen * mates, axis=0, keepdims=True)
        target = jnp.where(arrival < keep_count, own, mate)
        return (target == place).astype(jnp.float32)

    lands_one = lands(first, arrival_one)
    lands_two = lands(second, arrival_two)
    out[0:experts, :] = share_one * lands_one + share_two * lands_two
    out[experts : 2 * experts, :] = share_one * share_two * (lands_one - lands_two)
    out[2 * experts :, :] = first - second


def route(tokens, w_router, expert_ids, partner):
    tok_rows = tokens.shape[0]
    experts = w_router.shape[1]
    slot_count = min(tok_rows, 4 * tok_rows // experts)
    return pl.pallas_call(
        functools.partial(routing_kernel, experts, 3 * slot_count // 4),
        out_shape=shaped((3 * experts, tok_rows), jnp.float32),
        in_specs=[WHOLE] * 3 + [pl.BlockSpec(memory_space=pltpu.SMEM)],
        out_specs=WHOLE,
        name="route",
        cost_estimate=cost(1 << 20, 1 << 20),
    )(tokens, w_router.T, expert_ids.T, partner)


def tile_of(number, size):
    return pl.ds(pl.multiple_of(number * size, size), size)


class Mover:
    def __init__(self, sems):
        self.sems = sems
        self.used = 0

    def start(self, source, target):
        copy = pltpu.make_async_copy(source, target, self.sems.at[self.used])
        self.used += 1
        copy.start()
        return copy


def fetch_rows(mover, blocks, rows):
    count = blocks[0].shape[0]
    return [
        mover.start(block, rows.at[pl.ds(number * count, count), :])
        for number, block in enumerate(blocks)
    ]


def forward(blocks, w_gate, w_up, tile):
    number = len(blocks)
    tok_rows, features = blocks[0].shape
    count = number * tok_rows
    width = w_gate.shape[1]

    def body(*refs):
        pieces, refs = refs[:number], refs[number:]
        wg, wu, hid, sw, sg, everything, x, bg, bu, h, a, b, sems_in, sems_out = refs
        mover, outward = Mover(sems_in), Mover(sems_out)
        moves = fetch_rows(mover, pieces, x)
        tiles = [pl.ds(step * tile, tile) for step in range(width // tile)]
        copies = [
            (
                mover.start(wg.at[:, place], bg.at[:, place]),
                mover.start(wu.at[:, place], bu.at[:, place]),
            )
            for place in tiles
        ]
        for copy in moves:
            copy.wait()
        done = []
        for place, pair in zip(tiles, copies):
            for copy in pair:
                copy.wait()
            if pair is copies[-1]:
                done.append(outward.start(x, everything))
            gate = jnp.dot(x[...], bg[:, place], preferred_element_type=jnp.float32)
            up = jnp.dot(x[...], bu[:, place], preferred_element_type=jnp.float32)
            sigmoid_gate = jax.nn.sigmoid(gate)
            swished = gate * sigmoid_gate
            h[:, place] = (swished * up).astype(jnp.bfloat16)
            a[:, place] = swished.astype(jnp.bfloat16)
            b[:, place] = (up * sigmoid_gate * (1.0 + gate * (1.0 - sigmoid_gate))).astype(
                jnp.bfloat16
            )
        done += [outward.start(h, hid), outward.start(a, sw), outward.start(b, sg)]
        for copy in done:
            copy.wait()

    flat = pltpu.VMEM((count, width), jnp.bfloat16)
    weights = pltpu.VMEM((features, width), jnp.bfloat16)
    return pl.pallas_call(
        body,
        out_shape=(in_hbm((count, width)),) * 3 + (in_hbm((count, features)),),
        in_specs=[LEFT] * (number + 2),
        out_specs=(LEFT,) * 4,
        scratch_shapes=[
            pltpu.VMEM((count, features), jnp.bfloat16),
            weights,
            weights,
            flat,
            flat,
            flat,
            pltpu.SemaphoreType.DMA((number + 2 * (width // tile),)),
            pltpu.SemaphoreType.DMA((4,)),
        ],
        compiler_params=pltpu.CompilerParams(vmem_limit_bytes=40 << 20),
        name="forward",
        cost_estimate=cost(4 * count * features * width, 6 * features * width),
    )(*on_hbm(*blocks, w_gate, w_up))


def down(core, hidden, w_down, tile, pins):
    count, width = hidden.shape
    half = w_down.shape[1] // 2
    steps = half // tile
    hidden = after(hidden, pins)

    def body(core_ref, hid, wd, keep, send, h, bd, k, s, sems_in, sems_out):
        mover, outward = Mover(sems_in), Mover(sems_out)
        copies = [mover.start(hid, h), mover.start(wd, bd)]
        for copy in copies:
            copy.wait()
        me = core_ref[0]
        done = []
        for side, target, out in ((1 - me, s, send), (me, k, keep)):
            for step in range(steps):
                source = pl.ds(pl.multiple_of(side * half + step * tile, tile), tile)
                columns = pl.ds(step * tile, tile)
                target[:, columns] = jnp.dot(
                    h[...], bd[:, source], preferred_element_type=jnp.float32
                ).astype(jnp.bfloat16)
                done.append(outward.start(target.at[:, columns], out.at[:, columns]))
        for copy in done:
            copy.wait()

    part = pltpu.VMEM((count, half), jnp.bfloat16)
    return pl.pallas_call(
        body,
        out_shape=(in_vmem((count, half)), in_hbm((count, half))),
        in_specs=[pl.BlockSpec(memory_space=pltpu.SMEM)] + [LEFT] * 2,
        out_specs=(LEFT,) * 2,
        scratch_shapes=[
            pltpu.VMEM((count, width), jnp.bfloat16),
            pltpu.VMEM((width, 2 * half), jnp.bfloat16),
            part,
            part,
            pltpu.SemaphoreType.DMA((2,)),
            pltpu.SemaphoreType.DMA((2 * steps,)),
        ],
        compiler_params=pltpu.CompilerParams(vmem_limit_bytes=24 << 20),
        name="down",
        cost_estimate=cost(4 * count * half * width, 4 * half * width),
    )(core, *on_hbm(hidden, w_down))


def backward(blocks, w_down, hidden, sw, sg, weight, slope, tile):
    number = len(blocks)
    tok_rows, features = blocks[0].shape
    count = number * tok_rows
    width = w_down.shape[0]

    def body(*refs):
        pieces, refs = refs[:number], refs[number:]
        wd, hid, swished, slopes, c, v, up_out, gate_out, hidden_out, ds, everything = refs[:11]
        x, bd, h, a, b, ug, gg, hc, sems_in, sems_out = refs[11:]
        mover, outward = Mover(sems_in), Mover(sems_out)
        moves = fetch_rows(mover, pieces, x)
        tiles = [pl.ds(step * tile, tile) for step in range(width // tile)]
        copies = [mover.start(wd.at[tiles[0], :], bd.at[tiles[0], :])]
        for copy in moves:
            copy.wait()
        rest = [mover.start(hid, h), mover.start(swished, a), mover.start(slopes, b)]
        ds[...] = jnp.zeros_like(ds)
        scale = c[...]
        for step, place in enumerate(tiles):
            if step + 1 < len(tiles):
                following = tiles[step + 1]
                copies.append(mover.start(wd.at[following, :], bd.at[following, :]))
            copies[step].wait()
            if step == 0:
                done = [outward.start(x, everything)]
            back = lax.dot_general(x[...], bd[place, :], NT, preferred_element_type=jnp.float32)
            if step == 0:
                for copy in rest:
                    copy.wait()
            value = h[:, place].astype(jnp.float32)
            ds[...] += jnp.sum(value * back, axis=1, keepdims=True) * v[...]
            hc[:, place] = (value * scale).astype(jnp.bfloat16)
            back = back * scale
            ug[:, place] = (back * a[:, place].astype(jnp.float32)).astype(jnp.bfloat16)
            gg[:, place] = (back * b[:, place].astype(jnp.float32)).astype(jnp.bfloat16)
        done += [
            outward.start(ug, up_out),
            outward.start(gg, gate_out),
            outward.start(hc, hidden_out),
        ]
        for copy in done:
            copy.wait()

    flat = pltpu.VMEM((count, width), jnp.bfloat16)
    return pl.pallas_call(
        body,
        out_shape=(in_hbm((count, width)),) * 3
        + (shaped((count, 1), jnp.float32), in_hbm((count, features))),
        in_specs=[LEFT] * (number + 4) + [WHOLE] * 2,
        out_specs=(LEFT,) * 3 + (WHOLE, LEFT),
        scratch_shapes=[
            pltpu.VMEM((count, features), jnp.bfloat16),
            pltpu.VMEM((width, features), jnp.bfloat16),
        ]
        + [flat] * 6
        + [
            pltpu.SemaphoreType.DMA((number + width // tile + 3,)),
            pltpu.SemaphoreType.DMA((4,)),
        ],
        compiler_params=pltpu.CompilerParams(vmem_limit_bytes=40 << 20),
        name="backward",
        cost_estimate=cost(2 * count * features * width, 2 * features * width),
    )(*on_hbm(*blocks, w_down, hidden, sw, sg), weight, slope)


def rows_back(core, gate_grad, up_grad, w_gate, w_up, first, last, tile, pins, rider=None):
    count, width = gate_grad.shape
    half = w_gate.shape[0] // 2
    gate_grad = after(gate_grad, pins)
    steps = (last - first) // tile

    riders = [] if rider is None else [rider]
    tail = TAIL * len(riders)

    def body(core_ref, gate_in, up_in, wg, wu, *refs):
        keep, send, gg, ug, bg, bu, k, s, sems_in, sems_out = refs[len(riders) :]
        if riders:
            s[count:, : rider.shape[1]] = pack(refs[0][...])
        mover, outward = Mover(sems_in), Mover(sems_out)
        me = core_ref[0]
        pieces = []
        for side, target, out in ((1 - me, s, send), (me, k, keep)):
            for step in range(steps):
                source = pl.ds(pl.multiple_of(side * half + first + step * tile, tile), tile)
                pieces.append((source, target, pl.ds(step * tile, tile), out))
        copies = []

        def load(number):
            if number < len(pieces):
                source, place = pieces[number][0], pl.ds(number * tile, tile)
                copies.append(mover.start(wg.at[source, :], bg.at[place, :]))
                copies.append(mover.start(wu.at[source, :], bu.at[place, :]))

        rows = [mover.start(gate_in, gg), mover.start(up_in, ug)]
        load(0)
        for copy in rows:
            copy.wait()
        done = []
        for number, (_, target, columns, out) in enumerate(pieces):
            load(number + 1)
            place = pl.ds(number * tile, tile)
            copies[2 * number].wait()
            total = lax.dot_general(gg[...], bg[place, :], NT, preferred_element_type=jnp.float32)
            copies[2 * number + 1].wait()
            total = total + lax.dot_general(
                ug[...], bu[place, :], NT, preferred_element_type=jnp.float32
            )
            target[:count, columns] = total.astype(jnp.bfloat16)
            done.append(outward.start(target.at[:, columns], out.at[:, columns]))
        for copy in done:
            copy.wait()

    flat = pltpu.VMEM((count, width), jnp.bfloat16)
    weights = pltpu.VMEM((2 * (last - first), width), jnp.bfloat16)
    part = pltpu.VMEM((count, last - first), jnp.bfloat16)
    sent = (count + tail, last - first)
    return pl.pallas_call(
        body,
        out_shape=((in_hbm if riders else in_vmem)((count, last - first)), in_hbm(sent)),
        in_specs=[pl.BlockSpec(memory_space=pltpu.SMEM)] + [LEFT] * 4 + [WHOLE] * len(riders),
        out_specs=(LEFT,) * 2,
        scratch_shapes=[flat, flat, weights, weights, part, pltpu.VMEM(sent, jnp.bfloat16)]
        + [pltpu.SemaphoreType.DMA((4 * steps + 2,)), pltpu.SemaphoreType.DMA((2 * steps,))],
        compiler_params=pltpu.CompilerParams(vmem_limit_bytes=40 << 20),
        name="rows_back",
        cost_estimate=cost(8 * count * (last - first) * width, 8 * (last - first) * width),
    )(core, *on_hbm(gate_grad, up_grad, w_gate, w_up), *riders)


def outer(left, right, pins):
    left = after(left, pins)
    return lax.dot_general(left, right, TN, preferred_element_type=jnp.float32).astype(jnp.bfloat16)


def small_call(body, outs, args, pins, name):
    first = after(args[0], pins)
    return pl.pallas_call(
        body,
        out_shape=tuple(outs),
        in_specs=[WHOLE] * len(args),
        out_specs=(WHOLE,) * len(outs),
        compiler_params=settings(),
        name=name,
        cost_estimate=cost(1 << 20, 1 << 20),
    )(first, *args[1:])


def add(one, two):
    return (one.astype(jnp.float32) + two.astype(jnp.float32)).astype(jnp.bfloat16)


def trade(values, kind):
    cores, experts = lax.axis_size("dp"), lax.axis_size("expert")
    pairs = []
    for core in range(cores):
        for place in range(experts):
            flip = {"peer": 0, "first": 1 + core, "second": 2 - core, "both": 3}[kind]
            other = core ^ 1 if kind == "peer" else core
            pairs.append((core * experts + place, other * experts + (place ^ flip)))
    return lax.ppermute(values, ("dp", "expert"), pairs)


TAIL = 16


def pack(values):
    count, length = values.shape
    row = lax.broadcasted_iota(jnp.int32, (TAIL, length), 0)
    out = jnp.zeros((TAIL, length), jnp.float32)
    for number, piece in enumerate(split3(values)):
        for place in range(count):
            line = piece[place : place + 1, :].astype(jnp.float32)
            out = jnp.where(row == number * count + place, line, out)
    return out.astype(jnp.bfloat16)


def unpack(block, count):
    block = block.astype(jnp.float32)
    row = lax.broadcasted_iota(jnp.int32, block.shape, 0)
    line = lax.broadcasted_iota(jnp.int32, (count, block.shape[1]), 0)
    out = jnp.zeros((count, block.shape[1]), jnp.float32)
    for place in range(count):
        picked = (row == place) | (row == count + place) | (row == 2 * count + place)
        total = jnp.sum(jnp.where(picked, block, 0.0), axis=0, keepdims=True)
        out = jnp.where(line == place, total, out)
    return out


class Reduction:
    def __init__(self, keep, send, tok_rows, odd, rider=None):
        self.rows = tok_rows
        self.width = keep.shape[1]
        self.keep = (keep,)
        self.odd = odd
        self.rider = rider
        self.arrived = (trade(send, "peer"),)

    def spread_part(self, number, pins):
        rows = self.rows

        def body(inputs, sent, kept):
            keep, arrived = inputs
            for side in range(2):
                for place, there in enumerate((0, 2, 1, 3)):
                    away = place in ((1, 3), (2, 3))[number]
                    slot = 2 * side + (place // 2, place % 2)[number]
                    (sent if away else kept)[0][pl.ds(slot * rows, rows), :] = add(
                        keep[pl.ds((4 * side + place) * rows, rows), :],
                        arrived[pl.ds((4 * (1 - side) + there) * rows, rows), :],
                    )

        shape = (4 * rows, self.width)
        sent = self.run(body, [shape], [shape], [], pins, "spread_part", True)
        self.arrived = (trade(sent[0], ("first", "second")[number]),)
        return list(self.keep)

    def cross_part(self, number, pins):
        rows = self.rows

        def body(inputs, sent, kept):
            keep, arrived = inputs
            for place in range(4):
                out = (sent if place % 2 else kept)[0]
                source = pl.ds(place * rows, rows)
                out[pl.ds(place // 2 * rows, rows), :] = add(keep[source, :], arrived[source, :])

        shape = (2 * rows, self.width)
        sent = self.run(body, [shape], [shape], [], pins, "cross_part", True)
        self.arrived = (trade(sent[0], ("second", "first")[number]),)
        return list(self.keep)

    def halve_part(self, pins):
        rows, half = 2 * self.rows, self.width // 2

        def body(inputs, sent, kept):
            one = add(inputs[0][:, :half], inputs[1][:rows, :half])
            two = add(inputs[0][:, half:], inputs[1][:rows, half:])
            flag = inputs[2][...] > 0
            sent[0][:rows, :] = jnp.where(flag, one, two)
            kept[0][...] = jnp.where(flag, two, one)

        shape = (rows, half)
        sent = self.run(body, [shape], [shape], [self.odd], pins, "halve_part", True)
        self.arrived = (swap(sent[0], "mp", 1),)
        return list(self.keep)

    def run(self, body, sent, kept, extra, pins, name, rides):
        riding = self.rider is not None
        outs = [
            shaped((rows + (TAIL if riding and number == 0 else 0), width))
            for number, (rows, width) in enumerate(sent)
        ]
        outs += [shaped(shape) for shape in kept]
        args = [*self.keep, *self.arrived, *extra]
        tail_at = len(self.keep)
        if riding:
            args.append(self.rider)
            outs.append(shaped(self.rider.shape, jnp.float32))

        def whole(*refs):
            inputs, outputs = refs[: len(args)], refs[len(args) :]
            given = inputs[:-1] if riding else inputs
            body(given, outputs[: len(sent)], outputs[len(sent) : len(sent) + len(kept)])
            if riding:
                total = inputs[-1][...]
                length = total.shape[1]
                if rides:
                    arrived = inputs[tail_at]
                    block = arrived[arrived.shape[0] - TAIL :, :length]
                    total = total + unpack(block, total.shape[0])
                outputs[-1][...] = total
                outputs[0][sent[0][0] :, :length] = pack(total)

        outs = small_call(whole, outs, args, pins, name)
        if riding:
            self.rider = outs[-1]
        self.keep = outs[len(sent) : len(sent) + len(kept)] if kept else (outs[0],)
        return outs[: len(sent)]

    def spread(self, pins, scale=None):
        rows, half = self.rows, self.width // 2

        def body(inputs, sent, kept):
            keep, arrived = inputs[0], inputs[1]
            for side in range(2):
                for place, there in enumerate((0, 2, 1, 3)):
                    source = pl.ds((4 * side + place) * rows, rows)
                    total = keep[source, :].astype(jnp.float32) + arrived[
                        pl.ds((4 * (1 - side) + there) * rows, rows), :
                    ].astype(jnp.float32)
                    if scale is not None:
                        total = total * inputs[2][source, :]
                    total = total.astype(jnp.bfloat16)
                    left = pl.ds((2 * side + place // 2) * rows, rows)
                    right = pl.ds((2 * side + place % 2) * rows, rows)
                    (sent if place in (1, 3) else kept)[0][left, :] = total[:, :half]
                    (sent if place in (2, 3) else kept)[1][right, :] = total[:, half:]

        extra = [] if scale is None else [scale]
        shape = (4 * rows, half)
        sent = self.run(body, [shape] * 2, [shape] * 2, extra, pins, "spread", False)
        self.arrived = (trade(sent[0], "first"), trade(sent[1], "second"))
        return list(self.keep[:1])

    def cross(self, pins):
        rows, half = self.rows, self.width // 2

        def body(inputs, sent, kept):
            for part in range(2):
                keep, arrived = inputs[part], inputs[2 + part]
                for place in range(4):
                    out = (sent if place % 2 else kept)[part]
                    source = pl.ds(place * rows, rows)
                    out[pl.ds(place // 2 * rows, rows), :] = add(
                        keep[source, :], arrived[source, :]
                    )

        shape = (2 * rows, half)
        sent = self.run(body, [shape] * 2, [shape] * 2, [], pins, "cross", True)
        self.arrived = (trade(sent[0], "second"), trade(sent[1], "first"))
        return list(self.keep[:1])

    def halve(self, pins):
        rows, half = 2 * self.rows, self.width // 2

        def body(inputs, sent, kept):
            one = add(inputs[0][...], inputs[2][:rows, :])
            two = add(inputs[1][...], inputs[3][...])
            flag = inputs[4][...] > 0
            sent[0][:rows, :] = jnp.where(flag, one, two)
            kept[0][...] = jnp.where(flag, two, one)

        shape = (rows, half)
        sent = self.run(body, [shape], [shape], [self.odd], pins, "halve", True)
        self.arrived = (swap(sent[0], "mp", 1),)
        return list(self.keep)

    def step(self, flip, pins):
        rows, half = 2 * self.rows, self.width // 2

        def body(inputs, sent, kept):
            sent[0][:rows, :] = add(inputs[0][:rows, :], inputs[1][:rows, :])

        sent = self.run(body, [(rows, half)], [], [], pins, "step", True)
        self.arrived = (swap(sent[0], "mp", flip),)
        return list(self.keep)

    def join(self, pins):
        rows, half = self.rows, self.width // 2

        def body(inputs, sent, kept):
            keep, arrived = inputs[0], inputs[1]
            flag = inputs[2][...] > 0
            for out, place in ((kept[0], pl.ds(0, rows)), (sent[0], pl.ds(rows, rows))):
                out[:rows, :half] = jnp.where(flag, arrived[place, :], keep[place, :])
                out[:rows, half:] = jnp.where(flag, keep[place, :], arrived[place, :])

        shape = (rows, self.width)
        sent = self.run(body, [shape], [shape], [self.odd], pins, "join", False)
        self.arrived = (trade(sent[0], "peer"),)
        return list(self.keep)


def meet(sums, pins):
    sizes = [len(item.arrived) for item in sums]
    held = lax.optimization_barrier(
        (*[array for item in sums for array in item.arrived], *pins)
    )
    for item, size in zip(sums, sizes):
        item.arrived, held = held[:size], held[size:]


def finish(parts, core, extra, pins, name):
    rows, width = parts[0].keep[0].shape
    features = 2 * width * len(parts)
    args = [item for part in parts for item in (part.keep[0], part.arrived[0])]
    at = len(args)
    args += [core, *extra]

    def body(*refs):
        out = refs[len(args)]
        flag = refs[at][...] > 0
        for number in range(len(parts)):
            keep, arrived = refs[2 * number][...], refs[2 * number + 1][:rows, :]
            sides = (jnp.where(flag, arrived, keep), jnp.where(flag, keep, arrived))
            for side, values in enumerate(sides):
                columns = pl.ds(side * features // 2 + number * width, width)
                if extra:
                    values = values.astype(jnp.float32)
                    logits, router = refs[at + 1], refs[at + 2]
                    for expert in range(router.shape[0]):
                        values = values + logits[:, expert : expert + 1] * (
                            router[expert : expert + 1, columns]
                        )
                out[:, columns] = values.astype(jnp.bfloat16)

    return small_call(body, [shaped((rows, features))], args, pins, name)[0]


def gather_rows(block, peer, near, second, far):
    near_peer, second_peer = trade(second, "peer"), trade(near, "peer")
    return [block, near, second, far, peer, near_peer, second_peer, trade(far, "peer")]


def swapped(blocks):
    return jnp.stack([blocks[0], blocks[2], blocks[1], blocks[3]])


def gather_small(small):
    found = jnp.stack([small, trade(small, "first")])
    return jnp.concatenate([found, trade(found, "second")], axis=0)


def order():
    core, expert = lax.axis_index("dp"), lax.axis_index("expert")
    flips = (0, 1 + core, 2 - core, 3)
    places = [(core ^ side) * 4 + (expert ^ flip) for side in range(2) for flip in flips]
    places = jnp.stack([jnp.asarray(place, jnp.int32) for place in places])
    return (lax.iota(jnp.int32, 8)[:, None] == places[None, :]).astype(jnp.float32)


def local_pairs(tokens, w_router, expert_ids, partner, gate_weight, up_weight, down_weight, grad_out):
    tok_rows, features = tokens.shape
    experts = w_router.shape[1]
    width = gate_weight.shape[2]
    w_gate, w_up, w_down = gate_weight[0], up_weight[0], down_weight[0]
    odd = (lax.axis_index("mp") & 1).astype(jnp.int32).reshape(1, 1)
    core = lax.axis_index("dp").astype(jnp.int32).reshape(1)

    tok_near = trade(tokens, "first")
    tok_second = trade(tokens, "second")
    tok_peer = trade(tokens, "peer")
    small = route(tokens, w_router, expert_ids, partner)
    tok_far = trade(after(tok_near, [small]), "second")
    small = gather_small(small)
    small_peer = trade(small, "peer")
    token_blocks = gather_rows(tokens, tok_peer, tok_near, tok_second, after(tok_far, [small]))
    later = after(grad_out, [tok_far])
    out_near = trade(later, "first")
    out_second = trade(later, "second")
    out_far = trade(later, "both")
    out_peer = trade(grad_out, "peer")
    small = jnp.concatenate([small, swapped(small_peer)], axis=0)
    mine = (lax.iota(jnp.int32, experts) == lax.axis_index("expert")).astype(jnp.float32)
    mine = mine[None, :, None]
    weight = jnp.sum(small[:, :experts] * mine, axis=1).reshape(-1, 1)
    slope = jnp.sum(small[:, experts : 2 * experts] * mine, axis=1).reshape(-1, 1)
    token_blocks[0] = after(token_blocks[0], [weight, slope])
    hidden, sw, sg, all_tokens = forward(token_blocks, w_gate, w_up, width // 4)
    keep, send = down(core, hidden, w_down, features // 4, [])
    out_near, out_second, out_far = (
        after(item, [keep]) for item in (out_near, out_second, out_far)
    )
    grad_blocks = gather_rows(grad_out, out_peer, out_near, out_second, out_far)
    send = after(send, [out_near, out_second, out_far])
    mixed = Reduction(keep, send, tok_rows, odd)
    grad_blocks[0] = after(grad_blocks[0], mixed.spread([], weight))
    up_grad, gate_grad, hidden, dshare, all_grads = backward(
        grad_blocks, w_down, hidden, sw, sg, weight, slope, width // 2
    )
    places = order()
    dlogit = jnp.sum(places[:, :, None] * dshare.reshape(1, -1, tok_rows), axis=1)
    dlogit = dlogit.reshape(2, -1)
    meet([mixed], [gate_grad])
    pins = mixed.cross([])
    half = features // 2
    middle = half // 2
    tile = middle
    keep, send = rows_back(
        core, gate_grad, up_grad, w_gate, w_up, 0, middle, tile, pins, dlogit
    )
    meet([mixed], [keep])
    pins = mixed.halve([])
    left = Reduction(keep, after(send, pins), tok_rows, odd, dlogit)
    keep, send = rows_back(core, gate_grad, up_grad, w_gate, w_up, middle, half, tile, pins)
    meet([mixed, left], [keep])
    pins = left.spread_part(0, [])
    right = Reduction(keep, after(send, pins), tok_rows, odd)
    pins = mixed.step(2, pins)
    pins = pins + right.spread_part(1, [])
    grad_down = outer(hidden, all_grads, pins)
    meet([left, right, mixed], [grad_down])
    pins = left.cross_part(0, []) + right.cross_part(1, [])
    pins = mixed.step(1, pins)
    grad_gate = outer(all_tokens, gate_grad, pins)
    meet([left, right, mixed], [grad_gate])
    pins = left.halve_part([]) + right.halve_part([])
    pins = mixed.join(pins)
    grad_up = outer(all_tokens, up_grad, pins)
    meet([left, right], [grad_up])
    pins = left.step(2, []) + right.step(2, [])
    side = core.reshape(1, 1)
    mixed_out = finish([mixed], side, (), pins, "finish_mixed")
    meet([left, right], [mixed_out])
    left.step(1, [])
    right.step(1, [])
    dlogit = left.rider.reshape(-1, tok_rows)
    left.rider = None
    dlogit = jnp.sum(places[:, :, None] * dlogit[:, None, :], axis=0)
    sign = jnp.swapaxes(small[:, 2 * experts :], 1, 2)
    grad_logits = (sign * dlogit[:, :, None]).reshape(-1, experts)
    pieces = jnp.concatenate(split3(grad_logits), axis=1)
    grad_router = jnp.einsum("rd,re->de", all_tokens, pieces, preferred_element_type=jnp.float32)
    grad_router = (
        grad_router[:, 2 * experts :] + grad_router[:, experts : 2 * experts]
    ) + grad_router[:, :experts]
    meet([left, right], [grad_router])
    left.join([])
    right.join([])
    extra = (grad_logits[:tok_rows], w_router.T)
    grad_tokens = finish([left, right], side, extra, [], "finish_tokens")
    return mixed_out, grad_tokens, grad_router, grad_gate[None], grad_up[None], grad_down[None]


def in_pairs():
    return (
        lax.axis_size("dp") == 2 and lax.axis_size("expert") == 4 and lax.axis_size("mp") == 4
    )


def local(tokens, w_router, expert_ids, partner, gate_weight, up_weight, down_weight, grad_out):
    if in_pairs():
        return local_pairs(
            tokens, w_router, expert_ids, partner, gate_weight, up_weight, down_weight, grad_out
        )
    experts = w_router.shape[1]
    blocks = ("dp", "expert")
    all_tokens = lax.all_gather(tokens, blocks, axis=0, tiled=True)
    all_grads = lax.all_gather(grad_out, blocks, axis=0, tiled=True)
    weight, slope, sign = routing(tokens, w_router, expert_ids, partner)
    small = lax.all_gather(
        jnp.concatenate([weight, slope, sign], axis=1), blocks, axis=0, tiled=True
    )
    mine = (lax.iota(jnp.int32, experts) == lax.axis_index("expert")).astype(jnp.float32)
    weight_all = jnp.sum(small[:, :experts] * mine, axis=1, keepdims=True)
    slope_all = jnp.sum(small[:, experts : 2 * experts] * mine, axis=1)
    sign_all = small[:, 2 * experts :]

    w_gate = gate_weight[0]
    w_up = up_weight[0]
    w_down = down_weight[0]
    pre_gate = jnp.dot(all_tokens, w_gate, preferred_element_type=jnp.float32)
    pre_up = jnp.dot(all_tokens, w_up, preferred_element_type=jnp.float32)
    back = jnp.einsum("rd,fd->rf", all_grads, w_down, preferred_element_type=jnp.float32)
    sigmoid_gate = jax.nn.sigmoid(pre_gate)
    swished = pre_gate * sigmoid_gate
    hidden = swished * pre_up
    dshare = jnp.sum(hidden * back, axis=1)
    hidden = (weight_all * hidden).astype(jnp.bfloat16)
    dhidden = weight_all * back
    up_grad = (dhidden * swished).astype(jnp.bfloat16)
    gate_grad = (dhidden * pre_up * sigmoid_gate * (1.0 + pre_gate * (1.0 - sigmoid_gate))).astype(
        jnp.bfloat16
    )
    dlogit = lax.psum(slope_all * dshare, ("dp", "expert", "mp"))

    def collect(partial_value):
        own = lax.psum_scatter(
            partial_value.astype(jnp.bfloat16), blocks, scatter_dimension=0, tiled=True
        )
        return lax.psum(own, "mp")

    mixed = collect(jnp.dot(hidden, w_down, preferred_element_type=jnp.float32))
    row_grads = collect(
        jnp.einsum("rf,df->rd", gate_grad, w_gate, preferred_element_type=jnp.float32)
        + jnp.einsum("rf,df->rd", up_grad, w_up, preferred_element_type=jnp.float32)
    )
    grad_down = jnp.einsum("rf,rd->fd", hidden, all_grads, preferred_element_type=jnp.float32)
    grad_gate = jnp.einsum("rd,rf->df", all_tokens, gate_grad, preferred_element_type=jnp.float32)
    grad_up = jnp.einsum("rd,rf->df", all_tokens, up_grad, preferred_element_type=jnp.float32)

    grad_logits = sign_all * dlogit[:, None]
    pieces = jnp.concatenate(split3(grad_logits), axis=1)
    grad_router = jnp.einsum("rd,re->de", all_tokens, pieces, preferred_element_type=jnp.float32)
    grad_router = (
        grad_router[:, 2 * experts :] + grad_router[:, experts : 2 * experts]
    ) + grad_router[:, :experts]
    tok_rows = tokens.shape[0]
    block = lax.axis_index("dp") * lax.axis_size("expert") + lax.axis_index("expert")
    own_logits = lax.dynamic_slice_in_dim(grad_logits, block * tok_rows, tok_rows, 0)
    router_back = jnp.dot(own_logits, w_router.T, precision=lax.Precision.HIGHEST)
    grad_tokens = (router_back + row_grads.astype(jnp.float32)).astype(jnp.bfloat16)
    return (
        mixed,
        grad_tokens,
        grad_router,
        grad_gate.astype(jnp.bfloat16)[None],
        grad_up.astype(jnp.bfloat16)[None],
        grad_down.astype(jnp.bfloat16)[None],
    )


def solution(mesh):
    in_specs = (
        P(("dp", "expert"), None),
        P(),
        P(("dp", "expert"), None),
        P(),
        P("expert", None, ("dp", "mp")),
        P("expert", None, ("dp", "mp")),
        P("expert", ("dp", "mp"), None),
        P(("dp", "expert"), None),
    )
    out_specs = (
        P(("dp", "expert"), None),
        P(("dp", "expert"), None),
        P(),
        P("expert", None, ("dp", "mp")),
        P("expert", None, ("dp", "mp")),
        P("expert", ("dp", "mp"), None),
    )
    return jax.shard_map(local, mesh=mesh, in_specs=in_specs, out_specs=out_specs, check_vma=False)
```
